256 devices in a mesh: tgt: 8 (over x_lo, y), src: 32 (over z, x_hi, core).
Axes of the slice: x: 4 (x_hi: 2, x_lo: 2; x = x_hi * 2 + x_lo), y: 4, z: 8, core: 2. Of those that a mesh axis runs over, the one named last changes fastest.
Arguments:
- target_points: float32 [3, 32768], P(None, ('tgt', 'src')), may hold values from 0 to 1
- boundary: float32 [3, 32768], P(None, ('tgt', 'src')), may hold values from -6 to 6
- self_inverse: float32 [3, 3, 32768], P(None, None, ('tgt', 'src')), may hold values from -0.5 to 1.6, as said below
- near_ids: int32 [256, 8], P(('tgt', 'src')), may hold values from 0 to 255, as said below
- near_count: int32 [256], P(('tgt', 'src')), may hold values from 1 to 8, as said below
- source_points: float32 [3, 32768], P(None, ('tgt', 'src')), may hold values from 0 to 1
- area: float32 [32768], P(('tgt', 'src')), may hold values from 0.0027621358 to 0.022097087
- history: float32 [2, 3, 32768], P(None, None, ('tgt', 'src')), may hold values from -6 to 6
- near_tensor: float32 [9, 32768], P(None, ('tgt', 'src')), may hold values from -12 to 12
Outputs:
- new_density: float32 [3, 32768], P(None, ('tgt', 'src'))
The draws below stay inside these ranges and needn't reach their ends.
Inputs may be any that keep to these rules, and one draw needn't show every extreme that they name: `near_ids`: each row names 8 different source blocks. `near_count`: some target block uses all 8 entries of its list. `self_inverse`: diagonal entries lie between 0.4 and 1.6, the others between -0.5 and 0.5.
All inputs are finite; a program needn't handle non-finite values.
Results may differ from the reference program's by a relative error of at most 0.0003.
Values sent between devices are 32-bit elements; how exact they have to be, the bound alone decides.
A program may use at most 64 MiB of HBM per device.

```python
import math
import jax
import jax.numpy as jnp
from jax import lax

T_DEV = 128
S_DEV = 128
NEAR = 8
BLOCKS = 256
TARGETS = 32768
SOURCES = 32768


def draw_self_inverse(key, part):
    first, second = jax.random.split(jax.random.fold_in(key, 5))
    diag = jax.random.uniform(first, (3, TARGETS), jnp.float32, 0.6, 1.4)
    off = jax.random.uniform(second, (3, 3, TARGETS), jnp.float32, -0.35, 0.35)
    unit = jnp.eye(3, dtype=jnp.float32)[:, :, None]
    return off * (1.0 - unit) + unit * diag[None, :, :]


def draw_near_ids(key, part):
    keys = jax.random.split(jax.random.fold_in(key, 11), BLOCKS)

    def one_row(row_key):
        return jax.random.permutation(row_key, BLOCKS)[:NEAR].astype(jnp.int32)
    return jax.vmap(one_row)(keys)


def draw_near_count(key, part):
    first, second = jax.random.split(jax.random.fold_in(key, 23))
    counts = jax.random.randint(first, (BLOCKS,), 1, NEAR + 1, dtype=jnp.int32)
    chosen = jax.random.randint(second, (), 0, BLOCKS, dtype=jnp.int32)
    return jnp.where(jnp.arange(BLOCKS, dtype=jnp.int32) == chosen, NEAR, counts).astype(jnp.int32)


def block_scale(key, dims, cuts, least, top_value):
    def one(dim, shards_of):
        steps = jax.random.uniform(jax.random.fold_in(jax.random.fold_in(key, 6), dim), (shards_of,), jnp.float32, least / len(cuts), top_value / len(cuts))
        return jnp.repeat(jnp.exp(steps), dims[dim] // shards_of).reshape((-1,) + (1,) * (len(dims) - dim - 1))

    loudness = one(*cuts[0])
    for cut in cuts[1:]:
        loudness = loudness * one(*cut)
    return loudness


def scatter_about(stream_key, shape, deviation, limit, cuts=(), held_as=jnp.bfloat16):
    array = jax.random.normal(stream_key, shape, jnp.float32) * deviation
    if len(cuts) > 0:
        array = block_scale(stream_key, shape, cuts, -0.22, 0.18) * array
    return jnp.clip(array, min=-limit, max=limit).astype(held_as)


def setup_inputs(seed: int = 0) -> dict:
    key_of = jax.random.split(jax.random.key(seed), 10)
    return {
        "target_points": jnp.clip(1.0 * jax.random.uniform(key_of[0], (3, TARGETS), jnp.float32) ** block_scale(key_of[0], (3, TARGETS), ((1, 256),), -0.2, 0.2), 0.0, 1.0),
        "boundary": scatter_about(key_of[1], (3, TARGETS), 1.0, 6.0, ((1, 256),), jnp.float32),
        "self_inverse": draw_self_inverse(jax.random.fold_in(key_of[9], 71), 0),
        "near_ids": draw_near_ids(jax.random.fold_in(key_of[9], 71), 0),
        "near_count": draw_near_count(jax.random.fold_in(key_of[9], 71), 0),
        "source_points": jnp.clip(1.0 * jax.random.uniform(key_of[5], (3, SOURCES), jnp.float32) ** block_scale(key_of[5], (3, SOURCES), ((1, 256),), -0.2, 0.2), 0.0, 1.0),
        "area": jnp.clip(jnp.exp(math.log(0.022097087) - 2.0794415 * jax.random.uniform(key_of[6], (SOURCES,), jnp.float32) ** block_scale(key_of[6], (SOURCES,), ((0, 256),), -0.2, 0.2)), 0.0027621358, 0.022097087),
        "history": scatter_about(key_of[7], (2, 3, SOURCES), 1.0, 6.0, ((2, 256),), jnp.float32),
        "near_tensor": scatter_about(key_of[8], (9, SOURCES), 2.0, 12.0, ((1, 256),), jnp.float32),
    }


SOFT_CORE = 0.001
NEAR_RATE = 2.0

def pair_sum(targets, payload, weight):
    apart_x = targets[0][:, None] - payload[0][None, :]
    apart_y = targets[1][:, None] - payload[1][None, :]
    apart_z = targets[2][:, None] - payload[2][None, :]
    squared = apart_x * apart_x + apart_y * apart_y + apart_z * apart_z
    soft_sq = squared + SOFT_CORE
    radius = jnp.sqrt(soft_sq)
    inverse = 1.0 / radius
    slow_wave = jnp.exp(-0.75 * radius)
    mid_wave = slow_wave * slow_wave
    fast_wave = mid_wave * mid_wave
    amp_one = mid_wave * inverse
    amp_two = fast_wave * inverse
    proj_one = apart_x * payload[3][None, :] + apart_y * payload[4][None, :] + apart_z * payload[5][None, :]
    proj_two = apart_x * payload[6][None, :] + apart_y * payload[7][None, :] + apart_z * payload[8][None, :]
    radial = ((0.5 * slow_wave * inverse - amp_one) * proj_one + (0.5 * mid_wave * inverse - amp_two) * proj_two) / soft_sq
    nearness = jnp.exp(-NEAR_RATE * squared) * weight
    results = []
    for component, spread in enumerate((apart_x, apart_y, apart_z)):
        total = amp_one * payload[3 + component][None, :] + amp_two * payload[6 + component][None, :]
        total = total + nearness * payload[9 + component][None, :] + radial * spread
        results.append(lax.optimization_barrier(jnp.sum(total, axis=1)))
    return jnp.stack(results, axis=0)

def reference(target_points, boundary, self_inverse, near_ids, near_count, source_points, area, history, near_tensor):
    first = area[None, :] * history[0]
    second = area[None, :] * history[1]
    mixed = lax.optimization_barrier(jnp.sum(near_tensor.reshape(3, 3, SOURCES) * history[0][None, :, :], axis=1))
    corrected = area[None, :] * mixed
    payload = jnp.concatenate([source_points, first, second, corrected], axis=0)
    owner = jnp.arange(SOURCES, dtype=jnp.int32) // S_DEV
    block_ids = jnp.arange(BLOCKS, dtype=jnp.int32)
    grouped = target_points.reshape(3, BLOCKS, T_DEV).transpose(1, 0, 2)

    def per_block(item):
        points, listed, count = item
        live = (jnp.arange(NEAR, dtype=jnp.int32) < count).astype(jnp.float32)
        hits = (listed[:, None] == block_ids[None, :]).astype(jnp.float32)
        mask = lax.optimization_barrier(jnp.sum(hits * live[:, None], axis=0))
        weight = mask[owner]
        return pair_sum(points, payload, weight[None, :])
    field = lax.map(per_block, (grouped, near_ids, near_count))
    field = field.transpose(1, 0, 2).reshape(3, TARGETS)
    residual = boundary - field
    return lax.optimization_barrier(jnp.sum(self_inverse * residual[None, :, :], axis=1))
```

```python
import math

import jax
import jax.numpy as jnp
from jax import lax
from jax.experimental import pallas as pl
from jax.experimental.pallas import tpu as pltpu
from jax.sharding import PartitionSpec as P

SOFT_CORE = 0.001
NEAR_RATE = 2.0
SCALE = 0.75 * math.log2(math.e)
SOFT = SCALE * SCALE * SOFT_CORE

LINE = 16
PLANE = 16
NEAR = 8
LANES = 128
GROUPS = 4
STEPS = 16 // GROUPS
MESH = pl.DeviceIdType.MESH
f32 = jnp.float32
bf16 = jnp.bfloat16


def split3(value):
    high = value.astype(bf16).astype(f32)
    rest = value - high
    mid = rest.astype(bf16).astype(f32)
    return high, mid, rest - mid


def kernel(
    tp_ref,
    bnd_ref,
    inv_ref,
    ids_ref,
    cnt_ref,
    sp_ref,
    area_ref,
    hist_ref,
    nt_ref,
    out_ref,
    srcb,
    tgtb,
    nearb,
    part_send,
    part_recv,
    feat,
    lhs,
    rhs,
    xs,
    rows,
    pair_a,
    pair_b,
    acc_a,
    acc_b,
    res,
    nsel,
    xcol,
    nacc,
    line_send,
    line_recv,
    plane_send,
    plane_recv,
    near_send,
    near_recv,
    twin_send,
    twin_recv,
    back_send,
    back_recv,
):
    tgt, src = lax.axis_index("tgt"), lax.axis_index("src")
    z, x_hi, core = src // 4, lax.rem(src // 2, 2), lax.rem(src, 2)
    me_line = z * 2 + core
    me_plane = tgt * 2 + x_hi

    def line_device(j):
        return (tgt, (j // 2) * 4 + x_hi * 2 + lax.rem(j, 2))

    def plane_device(i):
        return (i // 2, z * 4 + lax.rem(i, 2) * 2 + core)

    def line_peer(k):
        k2 = k // 2
        off = ((k2 + 1) // 2) * (2 * lax.rem(k2, 2) - 1)
        return lax.rem(z + off + 8, 8) * 2 + lax.rem(core + k, 2)

    def plane_peer(k):
        return lax.rem(me_plane + k, PLANE)

    barrier = pltpu.get_barrier_semaphore()

    def greet(k, carry):
        pl.semaphore_signal(
            barrier, inc=1, device_id=line_device(line_peer(k)), device_id_type=MESH
        )
        pl.semaphore_signal(
            barrier, inc=1, device_id=plane_device(plane_peer(k)), device_id_type=MESH
        )
        return carry

    lax.fori_loop(1, LINE, greet, 0)

    area = area_ref[...]
    srcb[me_line, 0, 0:3, :] = sp_ref[...]
    h0, h1 = hist_ref[0], hist_ref[1]
    for a in range(3):
        mixed = jnp.sum(nt_ref[3 * a : 3 * a + 3, :] * h0, axis=0, keepdims=True)
        srcb[me_line, 0, 3 + a : 4 + a, :] = area * mixed
    srcb[me_line, 1, 0:3, :] = (area * h0) * SCALE
    srcb[me_line, 1, 3:6, :] = (area * h1) * SCALE
    tgtb[me_plane, 0:3, :] = tp_ref[...]

    def line_copy(slot, peer):
        return pltpu.make_async_remote_copy(
            src_ref=srcb.at[slot, :, 0:6, :],
            dst_ref=srcb.at[slot, :, 0:6, :],
            send_sem=line_send.at[peer],
            recv_sem=line_recv.at[slot],
            device_id=line_device(peer),
            device_id_type=MESH,
        )

    def plane_copy(slot, peer):
        return pltpu.make_async_remote_copy(
            src_ref=tgtb.at[slot, 0:3, :],
            dst_ref=tgtb.at[slot, 0:3, :],
            send_sem=plane_send.at[peer],
            recv_sem=plane_recv.at[slot],
            device_id=plane_device(peer),
            device_id_type=MESH,
        )

    half = pl.multiple_of(core * 8, 8)

    def near_copy(slot, peer):
        return pltpu.make_async_remote_copy(
            src_ref=srcb.at[pl.ds(half, 8), 0, 0:6, :],
            dst_ref=nearb.at[slot, pl.ds(half, 8), 0:6, :],
            send_sem=near_send.at[peer],
            recv_sem=near_recv.at[slot],
            device_id=plane_device(peer),
            device_id_type=MESH,
        )

    def twin_copy(which):
        part = nearb.at[:, pl.ds(pl.multiple_of(which * 8, 8), 8), 0:6, :]
        return pltpu.make_async_remote_copy(
            src_ref=part,
            dst_ref=part,
            send_sem=twin_send,
            recv_sem=twin_recv,
            device_id=(tgt, z * 4 + x_hi * 2 + 1 - core),
            device_id_type=MESH,
        )

    def back_copy(block, slot):
        return pltpu.make_async_remote_copy(
            src_ref=part_send.at[block, 0:3, :],
            dst_ref=part_recv.at[slot, 0:3, :],
            send_sem=back_send.at[block],
            recv_sem=back_recv.at[slot],
            device_id=plane_device(block),
            device_id_type=MESH,
        )

    pl.semaphore_wait(barrier, LINE - 1 + PLANE - 1)

    def send(k, carry):
        plane_copy(me_plane, plane_peer(k)).start()
        line_copy(me_line, line_peer(k)).start()
        return carry

    lax.fori_loop(1, LINE, send, 0)

    def prep_target(s):
        x = (tgtb[s, 0:3, :] - 0.5) * SCALE
        high, mid, low = split3(x)
        n_high, n_mid, n_low = split3(jnp.sum(x * x, axis=0, keepdims=True))
        feat[3, 0:3, :] = high
        feat[3, 3:6, :] = high
        feat[3, 6:9, :] = high
        feat[3, 9:12, :] = mid
        feat[3, 12:15, :] = mid
        feat[3, 15:18, :] = low
        feat[3, 18:19, :] = n_high
        feat[3, 19:20, :] = n_mid
        feat[3, 20:21, :] = n_low
        feat[3, 21:24, :] = jnp.ones((3, LANES), f32)
        lhs[s] = feat[3].T.astype(bf16)
        xs[s, 0:3, :] = x

    def prep_source(s):
        y = (srcb[s, 0, 0:3, :] - 0.5) * SCALE
        one, zero = jnp.ones((3, LANES), f32), jnp.zeros((3, LANES), f32)

        def put(number, parts, middle, tail):
            high, mid, low = parts
            feat[number, 0:3, :] = high
            feat[number, 3:6, :] = mid
            feat[number, 6:9, :] = low
            feat[number, 9:12, :] = high
            feat[number, 12:15, :] = mid
            feat[number, 15:18, :] = high
            feat[number, 18:21, :] = middle
            feat[number, 21:22, :] = tail[0]
            feat[number, 22:23, :] = tail[1]
            feat[number, 23:24, :] = tail[2]
            rhs[s, :, LANES * number : LANES * (number + 1)] = feat[number].astype(bf16)

        square = jnp.sum(y * y, axis=0, keepdims=True) + SOFT
        put(0, split3(-2.0 * y), one, split3(square))
        rows[s, 0:3, :] = y
        for n in range(2):
            dens = srcb[s, 1, 3 * n : 3 * n + 3, :]
            put(n + 1, split3(dens), zero, split3(-jnp.sum(y * dens, axis=0, keepdims=True)))
            rows[s, 3 + 3 * n : 6 + 3 * n, :] = dens

    for n in range(4):
        feat[n, 24:32, :] = jnp.zeros((8, LANES), f32)
    prep_target(me_plane)
    prep_source(me_line)

    def prep(k, carry):
        i, j = plane_peer(k), line_peer(k)
        plane_copy(i, i).wait_recv()
        prep_target(i)
        line_copy(j, j).wait_recv()
        prep_source(j)
        return carry

    lax.fori_loop(1, LINE, prep, 0)

    def send_near(k, carry):
        near_copy(me_plane, plane_peer(k)).start()
        return carry

    lax.fori_loop(1, PLANE, send_near, 0)

    def keep_near(k, carry):
        nearb[me_plane, half + k, 0:6, :] = srcb[half + k, 0, 0:6, :]
        return carry

    lax.fori_loop(0, 8, keep_near, 0)

    def generate(dst, block, step):
        left = lhs[block]
        for q in range(LINE // STEPS):
            s = step * (LINE // STEPS) + q
            dst[s] = jnp.dot(left, rhs[s], preferred_element_type=f32)

    def work(pair, acc, step):
        total = [[None] * 4 for _ in range(GROUPS)]
        for s in range(LINE):
            row = [rows[s, pl.ds(r, 8, stride=0), :] for r in range(9)]
            for g in range(GROUPS):
                r0 = pl.multiple_of((step * GROUPS + g) * 8, 8)
                soft = pair[s, pl.ds(r0, 8), 0:LANES]
                proj_1 = pair[s, pl.ds(r0, 8), LANES : 2 * LANES]
                proj_2 = pair[s, pl.ds(r0, 8), 2 * LANES : 3 * LANES]
                inv = lax.rsqrt(soft)
                wave = jnp.exp2(-(soft * inv))
                wave2 = wave * wave
                half_amp = wave * inv
                amp = half_amp * wave
                radial = (half_amp * (inv * inv)) * (
                    (0.5 - wave) * proj_1 + (wave * (0.5 - wave2)) * proj_2
                )
                terms = [
                    amp * (row[3 + c] + wave2 * row[6 + c]) - radial * row[c] for c in range(3)
                ]
                terms.append(radial)
                for c in range(4):
                    old = total[g][c]
                    total[g][c] = terms[c] if old is None else old + terms[c]
        for g in range(GROUPS):
            r0 = pl.multiple_of((step * GROUPS + g) * 8, 8)
            for c in range(4):
                acc[c, pl.ds(r0, 8), :] = total[g][c]

    def reduce_lanes(acc, c):
        res[c] = jnp.sum(acc[c].T, axis=0, keepdims=True)

    def block_of(n):
        return lax.rem(me_plane + 1 + n, PLANE)

    def finish(n):
        block = block_of(n)
        for c in range(3):
            part_send[block, c : c + 1, :] = res[c] + xs[block, c : c + 1, :] * res[3]

    def block_step(n, pair, following, acc, before):
        nxt = block_of(lax.rem(n + 1, PLANE))

        def step(it, carry):
            reduce_lanes(before, it)
            generate(following, nxt, it)
            work(pair, acc, it)
            return carry

        lax.fori_loop(0, STEPS, step, 0)

    def send_back(n):
        finish(n)
        back_copy(block_of(n), me_plane).start()

    def first(it, carry):
        generate(pair_a, block_of(0), it)
        return carry

    lax.fori_loop(0, STEPS, first, 0)

    def two(i, carry):
        block_step(2 * i, pair_a, pair_b, acc_a, acc_b)

        @pl.when(i > 0)
        def _():
            send_back(2 * i - 1)

        block_step(2 * i + 1, pair_b, pair_a, acc_b, acc_a)
        send_back(2 * i)

        @pl.when(i == 4)
        def _():
            def landed(k, c):
                peer = plane_peer(k)
                near_copy(peer, peer).wait_recv()
                return c

            lax.fori_loop(1, PLANE, landed, 0)
            twin_copy(core).start()

        return carry

    lax.fori_loop(0, PLANE // 2, two, 0)
    for c in range(4):
        reduce_lanes(acc_b, c)
    finish(PLANE - 1)

    for c in range(3):
        xcol[c] = jnp.broadcast_to(tp_ref[c : c + 1, :], (LANES, LANES)).T
    twin_copy(1 - core).wait_recv()
    for k in range(NEAR):
        listed = ids_ref[0, k]
        of_tgt, of_src = listed // 32, lax.rem(listed, 32)
        i = of_tgt * 2 + lax.rem(of_src // 2, 2)
        j = (of_src // 4) * 2 + lax.rem(of_src, 2)
        live = jnp.where(k < cnt_ref[0], 1.0, 0.0)
        piece = nearb[i, j, 0:6, :]
        nsel[k, 0:3, :] = piece[0:3]
        nsel[k, 3:6, :] = piece[3:6] * live

    def near_group(g, carry):
        r0 = pl.multiple_of(g * 8, 8)
        x = [xcol[c, pl.ds(r0, 8), :] for c in range(3)]
        total = [jnp.zeros((8, LANES), f32)] * 3
        for k in range(NEAR):
            row = [nsel[k, pl.ds(r, 8, stride=0), :] for r in range(6)]
            apart = [x[c] - row[c] for c in range(3)]
            square = apart[0] * apart[0] + apart[1] * apart[1] + apart[2] * apart[2]
            close = jnp.exp2(square * (-NEAR_RATE * math.log2(math.e)))
            total = [total[c] + close * row[3 + c] for c in range(3)]
        for c in range(3):
            nacc[c, pl.ds(r0, 8), :] = total[c]
        return carry

    lax.fori_loop(0, 16, near_group, 0)

    field = part_send[me_plane, 0:3, :]
    near = [jnp.sum(nacc[c].T, axis=0, keepdims=True) for c in range(3)]

    def gather_back(k, total):
        peer = plane_peer(k)
        back_copy(peer, peer).wait_recv()
        return total + part_recv[peer, 0:3, :]

    field = lax.fori_loop(1, PLANE, gather_back, field)
    left = [bnd_ref[c : c + 1, :] - (field[c : c + 1, :] + near[c]) for c in range(3)]
    for a in range(3):
        out_ref[a : a + 1, :] = (
            inv_ref[a, 0:1, :] * left[0] + inv_ref[a, 1:2, :] * left[1]
        ) + inv_ref[a, 2:3, :] * left[2]

    def sent(k, carry):
        i, j = plane_peer(k), line_peer(k)
        plane_copy(me_plane, i).wait_send()
        line_copy(me_line, j).wait_send()
        near_copy(me_plane, i).wait_send()
        back_copy(i, me_plane).wait_send()
        return carry

    lax.fori_loop(1, LINE, sent, 0)
    twin_copy(core).wait_send()


def per_device(tp, bnd, inv, ids, cnt, sp, area, hist, nt):
    vmem = pl.BlockSpec(memory_space=pltpu.VMEM)
    smem = pl.BlockSpec(memory_space=pltpu.SMEM)
    dma = pltpu.SemaphoreType.DMA
    return pl.pallas_call(
        kernel,
        out_shape=jax.ShapeDtypeStruct((3, LANES), f32),
        in_specs=[vmem, vmem, vmem, smem, smem, vmem, vmem, vmem, vmem],
        out_specs=vmem,
        scratch_shapes=[
            pltpu.VMEM((LINE, 2, 8, LANES), f32),
            pltpu.VMEM((PLANE, 8, LANES), f32),
            pltpu.VMEM((PLANE, LINE, 8, LANES), f32),
            pltpu.VMEM((PLANE, 8, LANES), f32),
            pltpu.VMEM((PLANE, 8, LANES), f32),
            pltpu.VMEM((4, 32, LANES), f32),
            pltpu.VMEM((PLANE, LANES, 32), bf16),
            pltpu.VMEM((LINE, 32, 3 * LANES), bf16),
            pltpu.VMEM((PLANE, 8, LANES), f32),
            pltpu.VMEM((LINE, 16, LANES), f32),
            pltpu.VMEM((LINE, LANES, 3 * LANES), f32),
            pltpu.VMEM((LINE, LANES, 3 * LANES), f32),
            pltpu.VMEM((4, LANES, LANES), f32),
            pltpu.VMEM((4, LANES, LANES), f32),
            pltpu.VMEM((4, 1, LANES), f32),
            pltpu.VMEM((NEAR, 8, LANES), f32),
            pltpu.VMEM((3, LANES, LANES), f32),
            pltpu.VMEM((3, LANES, LANES), f32),
            dma((LINE,)),
            dma((LINE,)),
            dma((PLANE,)),
            dma((PLANE,)),
            dma((PLANE,)),
            dma((PLANE,)),
            dma,
            dma,
            dma((PLANE,)),
            dma((PLANE,)),
        ],
        compiler_params=pltpu.CompilerParams(
            collective_id=0, has_side_effects=True, vmem_limit_bytes=48 * 1024 * 1024
        ),
    )(tp, bnd, inv, ids, cnt, sp, area.reshape(1, LANES), hist, nt)


def solution(mesh):
    placed = (
        P(None, ("tgt", "src")),
        P(None, ("tgt", "src")),
        P(None, None, ("tgt", "src")),
        P(("tgt", "src"), None),
        P(("tgt", "src")),
        P(None, ("tgt", "src")),
        P(("tgt", "src")),
        P(None, None, ("tgt", "src")),
        P(None, ("tgt", "src")),
    )
    return jax.shard_map(
        per_device, mesh=mesh, in_specs=placed, out_specs=P(None, ("tgt", "src")), check_vma=False
    )
```

```python
import math

import jax
import jax.numpy as jnp
from jax import lax
from jax.experimental import pallas as pl
from jax.experimental.pallas import tpu as pltpu
from jax.sharding import PartitionSpec as P

SOFT_CORE = 0.001
NEAR_RATE = 2.0
SCALE = 0.75 * math.log2(math.e)
SOFT = SCALE * SCALE * SOFT_CORE

LINE = 16
PLANE = 16
NEAR = 8
LANES = 128
GROUPS = 4
STEPS = 16 // GROUPS
ORDER = "00 03 01 30 10 33 31 13 11 02 20 32 12 23 21 22".split()


def digits(place):
    number = sum(int(step[place]) << (2 * n) for n, step in enumerate(ORDER))
    return number - (1 << 32) if number >= 1 << 31 else number


ORDER_X, ORDER_Y = digits(0), digits(1)
MESH = pl.DeviceIdType.MESH
f32 = jnp.float32
bf16 = jnp.bfloat16


def split3(value):
    high = value.astype(bf16).astype(f32)
    rest = value - high
    mid = rest.astype(bf16).astype(f32)
    return high, mid, rest - mid


def kernel(
    tp_hbm,
    bnd_hbm,
    inv_hbm,
    ids_hbm,
    cnt_hbm,
    sp_hbm,
    area_hbm,
    hist_hbm,
    nt_hbm,
    out_ref,
    tp_ref,
    bnd_ref,
    inv_ref,
    ids_ref,
    cnt_ref,
    sp_ref,
    area_ref,
    hist_ref,
    nt_ref,
    in_sem,
    srcb,
    tgtb,
    nearb,
    part_send,
    part_recv,
    feat,
    lhs,
    rhs,
    xs,
    rows,
    pair_a,
    pair_b,
    acc_a,
    acc_b,
    res,
    nsel,
    xcol,
    nacc,
    line_send,
    line_recv,
    plane_send,
    plane_recv,
    near_send,
    near_recv,
    twin_send,
    twin_recv,
    back_send,
    back_recv,
):
    tgt, src = lax.axis_index("tgt"), lax.axis_index("src")
    z, x_hi, core = src // 4, lax.rem(src // 2, 2), lax.rem(src, 2)
    me_line = z * 2 + core
    me_plane = tgt * 2 + x_hi

    def line_device(j):
        return (tgt, (j // 2) * 4 + x_hi * 2 + lax.rem(j, 2))

    def plane_device(i):
        return (i // 2, z * 4 + lax.rem(i, 2) * 2 + core)

    def line_peer(k):
        k2 = k // 2
        off = ((k2 + 1) // 2) * (2 * lax.rem(k2, 2) - 1)
        return lax.rem(z + off + 8, 8) * 2 + lax.rem(core + k, 2)

    def plane_peer(k):
        x = lax.rem(x_hi * 2 + tgt // 4 + ((ORDER_X >> (2 * k)) & 3), 4)
        y = lax.rem(tgt + ((ORDER_Y >> (2 * k)) & 3), 4)
        return (lax.rem(x, 2) * 4 + y) * 2 + x // 2

    barrier = pltpu.get_barrier_semaphore()

    def greet(k, carry):
        pl.semaphore_signal(
            barrier, inc=1, device_id=line_device(line_peer(LINE - k)), device_id_type=MESH
        )
        pl.semaphore_signal(
            barrier, inc=1, device_id=plane_device(plane_peer(PLANE - k)), device_id_type=MESH
        )
        return carry

    lax.fori_loop(1, LINE, greet, 0)

    early = [(tp_hbm, tp_ref), (sp_hbm, sp_ref), (area_hbm, area_ref)]
    early += [(hist_hbm, hist_ref), (nt_hbm, nt_ref)]
    late = [(bnd_hbm, bnd_ref), (inv_hbm, inv_ref), (ids_hbm, ids_ref), (cnt_hbm, cnt_ref)]
    loads = [
        pltpu.make_async_copy(a, b, in_sem.at[n]) for n, (a, b) in enumerate(early + late)
    ]
    for load in loads:
        load.start()
    for load in loads[: len(early)]:
        load.wait()

    area = area_ref[...]
    srcb[me_plane, 0, 0:3, :] = sp_ref[...]
    h0, h1 = hist_ref[:, 0, :], hist_ref[:, 1, :]
    for a in range(3):
        mixed = jnp.sum(nt_ref[3 * a : 3 * a + 3, :] * h0, axis=0, keepdims=True)
        srcb[me_plane, 0, 3 + a : 4 + a, :] = area * mixed
    srcb[me_plane, 1, 0:3, :] = (area * h0) * SCALE
    srcb[me_plane, 1, 3:6, :] = (area * h1) * SCALE
    tgtb[me_line, 0:3, :] = tp_ref[...]

    def line_copy(slot, peer):
        return pltpu.make_async_remote_copy(
            src_ref=tgtb.at[slot, 0:3, :],
            dst_ref=tgtb.at[slot, 0:3, :],
            send_sem=line_send.at[peer],
            recv_sem=line_recv.at[slot],
            device_id=line_device(peer),
            device_id_type=MESH,
        )

    def plane_copy(slot, peer):
        return pltpu.make_async_remote_copy(
            src_ref=srcb.at[slot, :, 0:6, :],
            dst_ref=srcb.at[slot, :, 0:6, :],
            send_sem=plane_send.at[peer],
            recv_sem=plane_recv.at[slot],
            device_id=plane_device(peer),
            device_id_type=MESH,
        )

    def near_copy(at_z, peer_z):
        return pltpu.make_async_remote_copy(
            src_ref=srcb.at[:, 0, 0:6, :],
            dst_ref=nearb.at[core, at_z, :, 0:6, :],
            send_sem=near_send.at[peer_z],
            recv_sem=near_recv.at[at_z],
            device_id=(tgt, peer_z * 4 + x_hi * 2 + core),
            device_id_type=MESH,
        )

    def twin_copy(which):
        part = nearb.at[which, :, :, 0:6, :]
        return pltpu.make_async_remote_copy(
            src_ref=part,
            dst_ref=part,
            send_sem=twin_send,
            recv_sem=twin_recv,
            device_id=(tgt, z * 4 + x_hi * 2 + 1 - core),
            device_id_type=MESH,
        )

    def back_copy(block, slot):
        return pltpu.make_async_remote_copy(
            src_ref=part_send.at[block, 0:3, :],
            dst_ref=part_recv.at[slot, 0:3, :],
            send_sem=back_send.at[block],
            recv_sem=back_recv.at[slot],
            device_id=line_device(block),
            device_id_type=MESH,
        )

    pl.semaphore_wait(barrier, LINE - 1 + PLANE - 1)

    def send(k, carry):
        plane_copy(me_plane, plane_peer(PLANE - k)).start()
        line_copy(me_line, line_peer(LINE - k)).start()
        return carry

    lax.fori_loop(1, LINE, send, 0)

    def prep_target(s):
        x = (tgtb[s, 0:3, :] - 0.5) * SCALE
        high, mid, low = split3(x)
        n_high, n_mid, n_low = split3(jnp.sum(x * x, axis=0, keepdims=True))
        feat[3, 0:3, :] = high
        feat[3, 3:6, :] = high
        feat[3, 6:9, :] = high
        feat[3, 9:12, :] = mid
        feat[3, 12:15, :] = mid
        feat[3, 15:18, :] = low
        feat[3, 18:19, :] = n_high
        feat[3, 19:20, :] = n_mid
        feat[3, 20:21, :] = n_low
        feat[3, 21:24, :] = jnp.ones((3, LANES), f32)
        lhs[s] = feat[3].T.astype(bf16)
        xs[s, 0:3, :] = x

    def prep_source(s):
        y = (srcb[s, 0, 0:3, :] - 0.5) * SCALE
        one, zero = jnp.ones((3, LANES), f32), jnp.zeros((3, LANES), f32)

        def put(number, parts, middle, tail):
            high, mid, low = parts
            feat[number, 0:3, :] = high
            feat[number, 3:6, :] = mid
            feat[number, 6:9, :] = low
            feat[number, 9:12, :] = high
            feat[number, 12:15, :] = mid
            feat[number, 15:18, :] = high
            feat[number, 18:21, :] = middle
            feat[number, 21:22, :] = tail[0]
            feat[number, 22:23, :] = tail[1]
            feat[number, 23:24, :] = tail[2]
            rhs[s, :, LANES * number : LANES * (number + 1)] = feat[number].astype(bf16)

        square = jnp.sum(y * y, axis=0, keepdims=True) + SOFT
        put(0, split3(-2.0 * y), one, split3(square))
        rows[s, 0:3, :] = y
        for n in range(2):
            dens = srcb[s, 1, 3 * n : 3 * n + 3, :]
            put(n + 1, split3(dens), zero, split3(-jnp.sum(y * dens, axis=0, keepdims=True)))
            rows[s, 3 + 3 * n : 6 + 3 * n, :] = dens

    for n in range(4):
        feat[n, 24:32, :] = jnp.zeros((8, LANES), f32)
    prep_target(me_line)
    prep_source(me_plane)

    def prep(k, carry):
        i, j = plane_peer(k), line_peer(k)
        line_copy(j, j).wait_recv()
        prep_target(j)
        plane_copy(i, i).wait_recv()
        prep_source(i)
        return carry

    lax.fori_loop(1, LINE, prep, 0)

    def send_near(k, carry):
        near_copy(z, lax.rem(z + k, 8)).start()
        return carry

    lax.fori_loop(1, 8, send_near, 0)

    def keep_near(i, carry):
        nearb[core, z, i, 0:6, :] = srcb[i, 0, 0:6, :]
        return carry

    lax.fori_loop(0, PLANE, keep_near, 0)

    def generate(dst, block, step):
        left = lhs[block]
        for q in range(LINE // STEPS):
            s = step * (LINE // STEPS) + q
            dst[s] = jnp.dot(left, rhs[s], preferred_element_type=f32)

    def work(pair, acc, step):
        total = [[None] * 4 for _ in range(GROUPS)]
        for s in range(LINE):
            row = [rows[s, pl.ds(r, 8, stride=0), :] for r in range(9)]
            for g in range(GROUPS):
                r0 = pl.multiple_of((step * GROUPS + g) * 8, 8)
                soft = pair[s, pl.ds(r0, 8), 0:LANES]
                proj_1 = pair[s, pl.ds(r0, 8), LANES : 2 * LANES]
                proj_2 = pair[s, pl.ds(r0, 8), 2 * LANES : 3 * LANES]
                inv = lax.rsqrt(soft)
                wave = jnp.exp2(-(soft * inv))
                wave2 = wave * wave
                half_amp = wave * inv
                amp = half_amp * wave
                radial = (half_amp * (inv * inv)) * (
                    (0.5 - wave) * proj_1 + (wave * (0.5 - wave2)) * proj_2
                )
                terms = [
                    amp * (row[3 + c] + wave2 * row[6 + c]) - radial * row[c] for c in range(3)
                ]
                terms.append(radial)
                for c in range(4):
                    old = total[g][c]
                    total[g][c] = terms[c] if old is None else old + terms[c]
        for g in range(GROUPS):
            r0 = pl.multiple_of((step * GROUPS + g) * 8, 8)
            for c in range(4):
                acc[c, pl.ds(r0, 8), :] = total[g][c]

    def reduce_lanes(acc, c):
        res[c] = jnp.sum(acc[c].T, axis=0, keepdims=True)

    def block_of(n):
        return line_peer(LINE - 1 - n)

    def finish(n):
        block = block_of(n)
        for c in range(3):
            part_send[block, c : c + 1, :] = res[c] + xs[block, c : c + 1, :] * res[3]

    def block_step(n, pair, following, acc, before):
        nxt = block_of(jnp.minimum(n + 1, PLANE - 1))

        def step(it, carry):
            reduce_lanes(before, it)
            generate(following, nxt, it)
            work(pair, acc, it)
            return carry

        lax.fori_loop(0, STEPS, step, 0)

    def send_back(n):
        finish(n)
        back_copy(block_of(n), me_line).start()

    def first(it, carry):
        generate(pair_a, block_of(0), it)
        return carry

    lax.fori_loop(0, STEPS, first, 0)

    def two(i, carry):
        block_step(2 * i, pair_a, pair_b, acc_a, acc_b)

        @pl.when(i > 0)
        def _():
            send_back(2 * i - 1)

        @pl.when(i == PLANE // 2 - 1)
        def _():
            for c in range(4):
                reduce_lanes(acc_a, c)
            send_back(2 * i)

        block_step(2 * i + 1, pair_b, pair_a, acc_b, acc_a)

        @pl.when(i < PLANE // 2 - 1)
        def _():
            send_back(2 * i)

        @pl.when(i == 5)
        def _():
            def landed(k, c):
                peer = lax.rem(z + k, 8)
                near_copy(peer, peer).wait_recv()
                return c

            lax.fori_loop(1, 8, landed, 0)
            twin_copy(core).start()

        return carry

    lax.fori_loop(0, PLANE // 2, two, 0)
    for c in range(4):
        reduce_lanes(acc_b, c)
    finish(PLANE - 1)

    for c in range(3):
        xcol[c] = jnp.broadcast_to(tp_ref[c : c + 1, :], (LANES, LANES)).T
    for load in loads[len(early) :]:
        load.wait()
    twin_copy(1 - core).wait_recv()
    for k in range(NEAR):
        listed = ids_ref[0, k]
        of_tgt, of_src = listed // 32, lax.rem(listed, 32)
        i = of_tgt * 2 + lax.rem(of_src // 2, 2)
        live = jnp.where(k < cnt_ref[0], 1.0, 0.0)
        piece = nearb[lax.rem(of_src, 2), of_src // 4, i, 0:6, :]
        nsel[k, 0:3, :] = piece[0:3]
        nsel[k, 3:6, :] = piece[3:6] * live

    def near_group(g, carry):
        r0 = pl.multiple_of(g * 8, 8)
        x = [xcol[c, pl.ds(r0, 8), :] for c in range(3)]
        total = [jnp.zeros((8, LANES), f32)] * 3
        for k in range(NEAR):
            row = [nsel[k, pl.ds(r, 8, stride=0), :] for r in range(6)]
            apart = [x[c] - row[c] for c in range(3)]
            square = apart[0] * apart[0] + apart[1] * apart[1] + apart[2] * apart[2]
            close = jnp.exp2(square * (-NEAR_RATE * math.log2(math.e)))
            total = [total[c] + close * row[3 + c] for c in range(3)]
        for c in range(3):
            nacc[c, pl.ds(r0, 8), :] = total[c]
        return carry

    lax.fori_loop(0, 16, near_group, 0)

    field = part_send[me_line, 0:3, :]
    near = [jnp.sum(nacc[c].T, axis=0, keepdims=True) for c in range(3)]

    def gather_back(k, total):
        peer = line_peer(k)
        back_copy(peer, peer).wait_recv()
        return total + part_recv[peer, 0:3, :]

    field = lax.fori_loop(1, PLANE, gather_back, field)
    left = [bnd_ref[c : c + 1, :] - (field[c : c + 1, :] + near[c]) for c in range(3)]
    for a in range(3):
        out_ref[a : a + 1, :] = (
            inv_ref[a, 0:1, :] * left[0] + inv_ref[a, 1:2, :] * left[1]
        ) + inv_ref[a, 2:3, :] * left[2]

    def sent(k, carry):
        i, j = plane_peer(k), line_peer(k)
        plane_copy(me_plane, i).wait_send()
        line_copy(me_line, j).wait_send()
        back_copy(j, me_line).wait_send()
        return carry

    lax.fori_loop(1, LINE, sent, 0)

    def near_sent(k, carry):
        near_copy(z, lax.rem(z + k, 8)).wait_send()
        return carry

    lax.fori_loop(1, 8, near_sent, 0)
    twin_copy(core).wait_send()


def per_device(tp, bnd, inv, ids, cnt, sp, area, hist, nt):
    vmem = pl.BlockSpec(memory_space=pltpu.VMEM)
    hbm = pl.BlockSpec(memory_space=pltpu.HBM)
    dma = pltpu.SemaphoreType.DMA
    return pl.pallas_call(
        kernel,
        out_shape=jax.ShapeDtypeStruct((3, LANES), f32),
        in_specs=[hbm] * 9,
        out_specs=vmem,
        scratch_shapes=[
            pltpu.VMEM((3, LANES), f32),
            pltpu.VMEM((3, LANES), f32),
            pltpu.VMEM((3, 3, LANES), f32),
            pltpu.SMEM((1, NEAR), jnp.int32),
            pltpu.SMEM((1,), jnp.int32),
            pltpu.VMEM((3, LANES), f32),
            pltpu.VMEM((1, LANES), f32),
            pltpu.VMEM((3, 2, LANES), f32),
            pltpu.VMEM((9, LANES), f32),
            dma((9,)),
            pltpu.VMEM((LINE, 2, 8, LANES), f32),
            pltpu.VMEM((PLANE, 8, LANES), f32),
            pltpu.VMEM((2, 8, PLANE, 8, LANES), f32),
            pltpu.VMEM((PLANE, 8, LANES), f32),
            pltpu.VMEM((PLANE, 8, LANES), f32),
            pltpu.VMEM((4, 32, LANES), f32),
            pltpu.VMEM((PLANE, LANES, 32), bf16),
            pltpu.VMEM((LINE, 32, 3 * LANES), bf16),
            pltpu.VMEM((PLANE, 8, LANES), f32),
            pltpu.VMEM((LINE, 16, LANES), f32),
            pltpu.VMEM((LINE, LANES, 3 * LANES), f32),
            pltpu.VMEM((LINE, LANES, 3 * LANES), f32),
            pltpu.VMEM((4, LANES, LANES), f32),
            pltpu.VMEM((4, LANES, LANES), f32),
            pltpu.VMEM((4, 1, LANES), f32),
            pltpu.VMEM((NEAR, 8, LANES), f32),
            pltpu.VMEM((3, LANES, LANES), f32),
            pltpu.VMEM((3, LANES, LANES), f32),
            dma((LINE,)),
            dma((LINE,)),
            dma((PLANE,)),
            dma((PLANE,)),
            dma((8,)),
            dma((8,)),
            dma,
            dma,
            dma((LINE,)),
            dma((LINE,)),
        ],
        compiler_params=pltpu.CompilerParams(
            collective_id=0, has_side_effects=True, vmem_limit_bytes=67043328
        ),
    )(
        tp, bnd, inv, ids, cnt, sp, area.reshape(1, LANES), hist.transpose(1, 0, 2), nt
    )


def solution(mesh):
    placed = (
        P(None, ("tgt", "src")),
        P(None, ("tgt", "src")),
        P(None, None, ("tgt", "src")),
        P(("tgt", "src"), None),
        P(("tgt", "src")),
        P(None, ("tgt", "src")),
        P(("tgt", "src")),
        P(None, None, ("tgt", "src")),
        P(None, ("tgt", "src")),
    )
    return jax.shard_map(
        per_device, mesh=mesh, in_specs=placed, out_specs=P(None, ("tgt", "src")), check_vma=False
    )
```

```python
import math

import jax
import jax.numpy as jnp
from jax import lax
from jax.experimental import pallas as pl
from jax.experimental.pallas import tpu as pltpu
from jax.sharding import PartitionSpec as P

SOFT_CORE = 0.001
NEAR_RATE = 2.0
SCALE = 0.75 * math.log2(math.e)
SOFT = SCALE * SCALE * SOFT_CORE

LINE = 16
PLANE = 16
NEAR = 8
LANES = 128
GROUPS = 4
ROWS = 8 * GROUPS
STEPS = LANES // ROWS
PLAN = ((0,), (8,), (1,), (9,), (2,), (10, 3), (11,), (4,), (12, 5), (13,), (6,), (7,)) + ((),) * 4
ORDER = (0, 3, 1, 30, 10, 33, 31, 13, 11, 2, 20, 32, 12, 23, 21, 22)


def digits(unit):
    number = sum((step // unit % 10) << (2 * n) for n, step in enumerate(ORDER))
    return number - (1 << 32) if number >= 1 << 31 else number


ORDER_X, ORDER_Y = digits(10), digits(1)
MESH = pl.DeviceIdType.MESH
f32 = jnp.float32
bf16 = jnp.bfloat16


def split3(value):
    high = value.astype(bf16).astype(f32)
    rest = value - high
    mid = rest.astype(bf16).astype(f32)
    return high, mid, rest - mid


def kernel(
    tp_hbm,
    bnd_hbm,
    inv_hbm,
    ids_hbm,
    cnt_hbm,
    sp_hbm,
    area_hbm,
    hist_hbm,
    nt_hbm,
    out_ref,
    tp_ref,
    bnd_ref,
    inv_ref,
    ids_ref,
    cnt_ref,
    sp_ref,
    area_ref,
    hist_ref,
    nt_ref,
    in_sem,
    srcb,
    tgtb,
    nearb,
    part_send,
    part_recv,
    feat,
    lhs,
    rhs_s,
    rhs_p,
    xs,
    rows,
    soft_a,
    soft_b,
    proj_a,
    proj_b,
    wave_a,
    wave_b,
    acc_a,
    acc_b,
    res,
    nsel,
    xcol,
    nacc,
    line_send,
    line_recv,
    plane_send,
    plane_recv,
    near_send,
    near_recv,
    twin_send,
    twin_recv,
    back_send,
    back_recv,
):
    tgt, src = lax.axis_index("tgt"), lax.axis_index("src")
    z, x_hi, core = src // 4, lax.rem(src // 2, 2), lax.rem(src, 2)
    me_line = z * 2 + core
    me_plane = tgt * 2 + x_hi

    def line_device(j):
        return (tgt, (j // 2) * 4 + x_hi * 2 + lax.rem(j, 2))

    def plane_device(i):
        return (i // 2, z * 4 + lax.rem(i, 2) * 2 + core)

    def line_peer(k):
        k2 = k // 2
        off = ((k2 + 1) // 2) * (2 * lax.rem(k2, 2) - 1)
        return lax.rem(z + off + 8, 8) * 2 + lax.rem(core + k, 2)

    def plane_peer(k):
        x = lax.rem(x_hi * 2 + tgt // 4 + ((ORDER_X >> (2 * k)) & 3), 4)
        y = lax.rem(tgt + ((ORDER_Y >> (2 * k)) & 3), 4)
        return (lax.rem(x, 2) * 4 + y) * 2 + x // 2

    barrier = pltpu.get_barrier_semaphore()

    def greet(k, carry):
        pl.semaphore_signal(
            barrier, inc=1, device_id=line_device(line_peer(LINE - k)), device_id_type=MESH
        )
        pl.semaphore_signal(
            barrier, inc=1, device_id=plane_device(plane_peer(PLANE - k)), device_id_type=MESH
        )
        return carry

    lax.fori_loop(1, LINE, greet, 0)

    early = [(tp_hbm, tp_ref), (sp_hbm, sp_ref), (area_hbm, area_ref)]
    early += [(hist_hbm, hist_ref), (nt_hbm, nt_ref)]
    late = [(bnd_hbm, bnd_ref), (inv_hbm, inv_ref), (ids_hbm, ids_ref), (cnt_hbm, cnt_ref)]
    loads = [
        pltpu.make_async_copy(a, b, in_sem.at[n]) for n, (a, b) in enumerate(early + late)
    ]
    for load in loads:
        load.start()
    for load in loads[: len(early)]:
        load.wait()

    area = area_ref[...]
    srcb[me_plane, 0, 0:3, :] = sp_ref[...]
    h0, h1 = hist_ref[:, 0, :], hist_ref[:, 1, :]
    for a in range(3):
        mixed = jnp.sum(nt_ref[3 * a : 3 * a + 3, :] * h0, axis=0, keepdims=True)
        srcb[me_plane, 0, 3 + a : 4 + a, :] = area * mixed
    srcb[me_plane, 1, 0:3, :] = (area * h0) * SCALE
    srcb[me_plane, 1, 3:6, :] = (area * h1) * SCALE
    tgtb[me_line, 0:3, :] = tp_ref[...]

    def line_copy(slot, peer):
        return pltpu.make_async_remote_copy(
            src_ref=tgtb.at[slot, 0:3, :],
            dst_ref=tgtb.at[slot, 0:3, :],
            send_sem=line_send.at[peer],
            recv_sem=line_recv.at[slot],
            device_id=line_device(peer),
            device_id_type=MESH,
        )

    def plane_copy(slot, peer):
        return pltpu.make_async_remote_copy(
            src_ref=srcb.at[slot, :, 0:6, :],
            dst_ref=srcb.at[slot, :, 0:6, :],
            send_sem=plane_send.at[peer],
            recv_sem=plane_recv.at[slot],
            device_id=plane_device(peer),
            device_id_type=MESH,
        )

    def near_copy(at_z, peer_z):
        return pltpu.make_async_remote_copy(
            src_ref=srcb.at[:, 0, 0:6, :],
            dst_ref=nearb.at[core, at_z, :, 0:6, :],
            send_sem=near_send.at[peer_z],
            recv_sem=near_recv.at[at_z],
            device_id=(tgt, peer_z * 4 + x_hi * 2 + core),
            device_id_type=MESH,
        )

    def twin_copy(which):
        part = nearb.at[which, :, :, 0:6, :]
        return pltpu.make_async_remote_copy(
            src_ref=part,
            dst_ref=part,
            send_sem=twin_send,
            recv_sem=twin_recv,
            device_id=(tgt, z * 4 + x_hi * 2 + 1 - core),
            device_id_type=MESH,
        )

    def back_copy(block, slot):
        return pltpu.make_async_remote_copy(
            src_ref=part_send.at[block, 0:3, :],
            dst_ref=part_recv.at[slot, 0:3, :],
            send_sem=back_send.at[block],
            recv_sem=back_recv.at[slot],
            device_id=line_device(block),
            device_id_type=MESH,
        )

    pl.semaphore_wait(barrier, LINE - 1 + PLANE - 1)

    def send(k, carry):
        plane_copy(me_plane, plane_peer(PLANE - k)).start()
        line_copy(me_line, line_peer(LINE - k)).start()
        return carry

    lax.fori_loop(1, LINE, send, 0)

    def prep_target(s, n):
        x = (tgtb[s, 0:3, :] - 0.5) * SCALE
        high, mid, low = split3(x)
        n_high, n_mid, n_low = split3(jnp.sum(x * x, axis=0, keepdims=True))
        feat[4, 0:3, :] = high
        feat[4, 3:6, :] = high
        feat[4, 6:9, :] = high
        feat[4, 9:12, :] = mid
        feat[4, 12:15, :] = mid
        feat[4, 15:18, :] = low
        feat[4, 18:19, :] = n_high
        feat[4, 19:20, :] = n_mid
        feat[4, 20:21, :] = n_low
        feat[4, 21:24, :] = jnp.ones((3, LANES), f32)
        lhs[n] = feat[4].T.astype(bf16)
        xs[n, 0:3, :] = x

    def prep_source(s):
        y = (srcb[s, 0, 0:3, :] - 0.5) * SCALE
        one, zero = jnp.ones((3, LANES), f32), jnp.zeros((3, LANES), f32)
        piece, place = s // 4, lax.rem(s, 4)

        def put(number, dst, base, value, middle, tail):
            high, mid, low = split3(value)
            t_high, t_mid, t_low = split3(tail)
            feat[number, 0:3, :] = high
            feat[number, 3:6, :] = mid
            feat[number, 6:9, :] = low
            feat[number, 9:12, :] = high
            feat[number, 12:15, :] = mid
            feat[number, 15:18, :] = high
            feat[number, 18:21, :] = middle
            feat[number, 21:22, :] = t_high
            feat[number, 22:23, :] = t_mid
            feat[number, 23:24, :] = t_low
            dst[piece, :, pl.ds(pl.multiple_of(base, LANES), LANES)] = feat[number].astype(bf16)

        square = jnp.sum(y * y, axis=0, keepdims=True) + SOFT
        put(0, rhs_s, place * LANES, -2.0 * y, one, square)
        rows[s, 0:3, :] = y
        first, second = srcb[s, 1, 0:3, :], srcb[s, 1, 3:6, :]
        for n, dens in enumerate((0.5 * first, 0.5 * second - first, second)):
            tail = -jnp.sum(y * dens, axis=0, keepdims=True)
            put(n + 1, rhs_p, place * (3 * LANES) + n * LANES, dens, zero, tail)
        rows[s, 3:6, :] = first
        rows[s, 6:9, :] = second

    for n in range(5):
        feat[n, 24:32, :] = jnp.zeros((8, LANES), f32)
    prep_target(me_line, LINE - 1)
    prep_source(me_plane)

    def prep(k, carry):
        i, j = plane_peer(k), line_peer(k)
        line_copy(j, j).wait_recv()
        prep_target(j, LINE - 1 - k)
        plane_copy(i, i).wait_recv()
        prep_source(i)
        return carry

    lax.fori_loop(1, LINE, prep, 0)

    def send_near(k, carry):
        near_copy(z, lax.rem(z + k, 8)).start()
        return carry

    lax.fori_loop(1, 8, send_near, 0)

    def keep_near(i, carry):
        nearb[core, z, i, 0:6, :] = srcb[i, 0, 0:6, :]
        return carry

    lax.fori_loop(0, PLANE, keep_near, 0)

    def distances(dst, block, it, q):
        left = lhs[block, pl.ds(pl.multiple_of(it * ROWS, ROWS), ROWS), :]
        right = rhs_s[q // 2, :, 256 * (q % 2) : 256 * (q % 2) + 256]
        dst[q] = jnp.dot(left, right, preferred_element_type=f32)

    def projections(dst, block, piece, q):
        right = rhs_p[piece, :, 256 * q : 256 * q + 256]
        dst[piece, :, 256 * q : 256 * q + 256] = jnp.dot(
            lhs[block], right, preferred_element_type=f32
        )

    def waves(soft, dst, s):
        lo = LANES * (s % 2)
        for g in range(GROUPS):
            value = soft[s // 2, 8 * g : 8 * g + 8, lo : lo + LANES]
            inv = lax.rsqrt(value)
            dst[0, s, 8 * g : 8 * g + 8, :] = inv
            dst[1, s, 8 * g : 8 * g + 8, :] = jnp.exp2(-(value * inv))

    def add_source(wave_ref, proj, s, r0, total):
        row = [rows[s, pl.ds(r, 8, stride=0), :] for r in range(9)]
        for g in range(GROUPS):
            inv, wave = (wave_ref[n, s, 8 * g : 8 * g + 8, :] for n in range(2))
            lo = 3 * LANES * (s % 4)
            half, cross, second = (
                proj[s // 4, pl.ds(r0 + 8 * g, 8), lo + LANES * n : lo + LANES * (n + 1)]
                for n in range(3)
            )
            wave2 = wave * wave
            ratio = wave * inv
            amp = ratio * wave
            radial = (ratio * (inv * inv)) * (half + wave * (cross - wave2 * second))
            terms = [
                amp * (row[3 + c] + wave2 * row[6 + c]) - radial * row[c] for c in range(3)
            ]
            terms.append(radial)
            for c in range(4):
                old = total[g][c]
                total[g][c] = terms[c] if old is None else old + terms[c]

    def reduce_lanes(acc, c):
        res[c] = jnp.sum(acc[c].T, axis=0, keepdims=True)

    def block_of(n):
        return line_peer(LINE - 1 - n)

    def finish(n):
        block = block_of(n)
        for c in range(3):
            part_send[block, c : c + 1, :] = res[c] + xs[n, c : c + 1, :] * res[3]

    def unit(n, it, wave_now, wave_next, soft_now, soft_next, proj, following, acc, before):
        r0 = pl.multiple_of(it * ROWS, ROWS)
        ahead = jnp.minimum(n * STEPS + it + 2, LINE * STEPS - 1)
        block_2, it_2 = ahead >> 2, ahead & (STEPS - 1)
        block_1 = jnp.minimum(n + 1, LINE - 1)
        total = [[None] * 4 for _ in range(GROUPS)]
        pad = 4 + (n & 1)
        for s in range(PLANE):
            waves(soft_now, wave_next, s)
            if s > 0:
                rhs_s[pad, 0:16, 0:LANES] = jnp.concatenate(
                    [total[0][0], total[1][1]], axis=0
                ).astype(bf16)
                rhs_p[pad, 0:16, 0:LANES] = jnp.concatenate(
                    [total[2][2], total[3][0]], axis=0
                ).astype(bf16)
            for tile in PLAN[s]:
                if tile < 8:
                    distances(soft_next, block_2, it_2, tile)
                else:
                    projections(following, block_1, it, tile - 8)
            if s == 4:
                reduce_lanes(before, it)
            add_source(wave_now, proj, s, r0, total)
        for g in range(GROUPS):
            for c in range(4):
                acc[c, pl.ds(r0 + 8 * g, 8), :] = total[g][c]

    def block_step(n, proj, following, acc, before):
        def two_units(j, carry):
            unit(n, 2 * j, wave_a, wave_b, soft_b, soft_a, proj, following, acc, before)
            unit(n, 2 * j + 1, wave_b, wave_a, soft_a, soft_b, proj, following, acc, before)
            return carry

        lax.fori_loop(0, STEPS // 2, two_units, 0)

    def send_back(n):
        finish(n)
        back_copy(block_of(n), me_line).start()

    for q in range(8):
        distances(soft_a, 0, 0, q)
        distances(soft_b, 0, 1, q)
    for piece in range(4):
        for q in range(6):
            projections(proj_a, 0, piece, q)
    for s in range(PLANE):
        waves(soft_a, wave_a, s)

    def two(i, carry):
        block_step(2 * i, proj_a, proj_b, acc_a, acc_b)

        @pl.when(i > 0)
        def _():
            send_back(2 * i - 1)

        @pl.when(i == PLANE // 2 - 1)
        def _():
            for c in range(4):
                reduce_lanes(acc_a, c)
            send_back(2 * i)

        block_step(2 * i + 1, proj_b, proj_a, acc_b, acc_a)

        @pl.when(i < PLANE // 2 - 1)
        def _():
            send_back(2 * i)

        @pl.when(i == 5)
        def _():
            def landed(k, c):
                peer = lax.rem(z + k, 8)
                near_copy(peer, peer).wait_recv()
                return c

            lax.fori_loop(1, 8, landed, 0)
            twin_copy(core).start()

        return carry

    lax.fori_loop(0, PLANE // 2, two, 0)
    for c in range(4):
        reduce_lanes(acc_b, c)
    finish(PLANE - 1)

    for c in range(3):
        xcol[c] = jnp.broadcast_to(tp_ref[c : c + 1, :], (LANES, LANES)).T
    for load in loads[len(early) :]:
        load.wait()
    twin_copy(1 - core).wait_recv()
    for k in range(NEAR):
        listed = ids_ref[0, k]
        of_tgt, of_src = listed // 32, lax.rem(listed, 32)
        i = of_tgt * 2 + lax.rem(of_src // 2, 2)
        live = jnp.where(k < cnt_ref[0], 1.0, 0.0)
        piece = nearb[lax.rem(of_src, 2), of_src // 4, i, 0:6, :]
        nsel[k, 0:3, :] = piece[0:3]
        nsel[k, 3:6, :] = piece[3:6] * live

    def near_group(g, carry):
        r0 = pl.multiple_of(g * 8, 8)
        x = [xcol[c, pl.ds(r0, 8), :] for c in range(3)]
        total = [jnp.zeros((8, LANES), f32)] * 3
        for k in range(NEAR):
            row = [nsel[k, pl.ds(r, 8, stride=0), :] for r in range(6)]
            apart = [x[c] - row[c] for c in range(3)]
            square = apart[0] * apart[0] + apart[1] * apart[1] + apart[2] * apart[2]
            close = jnp.exp2(square * (-NEAR_RATE * math.log2(math.e)))
            total = [total[c] + close * row[3 + c] for c in range(3)]
        for c in range(3):
            nacc[c, pl.ds(r0, 8), :] = total[c]
        return carry

    lax.fori_loop(0, 16, near_group, 0)

    field = part_send[me_line, 0:3, :]
    near = [jnp.sum(nacc[c].T, axis=0, keepdims=True) for c in range(3)]

    def gather_back(k, total):
        peer = line_peer(k)
        back_copy(peer, peer).wait_recv()
        return total + part_recv[peer, 0:3, :]

    field = lax.fori_loop(1, PLANE, gather_back, field)
    left = [bnd_ref[c : c + 1, :] - (field[c : c + 1, :] + near[c]) for c in range(3)]
    for a in range(3):
        out_ref[a : a + 1, :] = (
            inv_ref[a, 0:1, :] * left[0] + inv_ref[a, 1:2, :] * left[1]
        ) + inv_ref[a, 2:3, :] * left[2]

    def sent(k, carry):
        i, j = plane_peer(k), line_peer(k)
        plane_copy(me_plane, i).wait_send()
        line_copy(me_line, j).wait_send()
        back_copy(j, me_line).wait_send()
        return carry

    lax.fori_loop(1, LINE, sent, 0)

    def near_sent(k, carry):
        near_copy(z, lax.rem(z + k, 8)).wait_send()
        return carry

    lax.fori_loop(1, 8, near_sent, 0)
    twin_copy(core).wait_send()


def per_device(tp, bnd, inv, ids, cnt, sp, area, hist, nt):
    vmem = pl.BlockSpec(memory_space=pltpu.VMEM)
    hbm = pl.BlockSpec(memory_space=pltpu.HBM)
    dma = pltpu.SemaphoreType.DMA
    return pl.pallas_call(
        kernel,
        out_shape=jax.ShapeDtypeStruct((3, LANES), f32),
        in_specs=[hbm] * 9,
        out_specs=vmem,
        scratch_shapes=[
            pltpu.VMEM((3, LANES), f32),
            pltpu.VMEM((3, LANES), f32),
            pltpu.VMEM((3, 3, LANES), f32),
            pltpu.SMEM((1, NEAR), jnp.int32),
            pltpu.SMEM((1,), jnp.int32),
            pltpu.VMEM((3, LANES), f32),
            pltpu.VMEM((1, LANES), f32),
            pltpu.VMEM((3, 2, LANES), f32),
            pltpu.VMEM((9, LANES), f32),
            dma((9,)),
            pltpu.VMEM((LINE, 2, 8, LANES), f32),
            pltpu.VMEM((PLANE, 8, LANES), f32),
            pltpu.VMEM((2, 8, PLANE, 8, LANES), f32),
            pltpu.VMEM((PLANE, 8, LANES), f32),
            pltpu.VMEM((PLANE, 8, LANES), f32),
            pltpu.VMEM((5, 32, LANES), f32),
            pltpu.VMEM((PLANE, LANES, 32), bf16),
            pltpu.VMEM((6, 32, 4 * LANES), bf16),
            pltpu.VMEM((6, 32, 12 * LANES), bf16),
            pltpu.VMEM((PLANE, 8, LANES), f32),
            pltpu.VMEM((LINE, 16, LANES), f32),
            pltpu.VMEM((8, ROWS, 256), f32),
            pltpu.VMEM((8, ROWS, 256), f32),
            pltpu.VMEM((4, LANES, 12 * LANES), f32),
            pltpu.VMEM((4, LANES, 12 * LANES), f32),
            pltpu.VMEM((2, PLANE, ROWS, LANES), f32),
            pltpu.VMEM((2, PLANE, ROWS, LANES), f32),
            pltpu.VMEM((4, LANES, LANES), f32),
            pltpu.VMEM((4, LANES, LANES), f32),
            pltpu.VMEM((4, 1, LANES), f32),
            pltpu.VMEM((NEAR, 8, LANES), f32),
            pltpu.VMEM((3, LANES, LANES), f32),
            pltpu.VMEM((3, LANES, LANES), f32),
            dma((LINE,)),
            dma((LINE,)),
            dma((PLANE,)),
            dma((PLANE,)),
            dma((8,)),
            dma((8,)),
            dma,
            dma,
            dma((LINE,)),
            dma((LINE,)),
        ],
        compiler_params=pltpu.CompilerParams(
            collective_id=0, has_side_effects=True, vmem_limit_bytes=67043328
        ),
    )(
        tp, bnd, inv, ids, cnt, sp, area.reshape(1, LANES), hist.transpose(1, 0, 2), nt
    )


def solution(mesh):
    placed = (
        P(None, ("tgt", "src")),
        P(None, ("tgt", "src")),
        P(None, None, ("tgt", "src")),
        P(("tgt", "src"), None),
        P(("tgt", "src")),
        P(None, ("tgt", "src")),
        P(("tgt", "src")),
        P(None, None, ("tgt", "src")),
        P(None, ("tgt", "src")),
    )
    return jax.shard_map(
        per_device, mesh=mesh, in_specs=placed, out_specs=P(None, ("tgt", "src")), check_vma=False
    )
```

```python
import math

import jax
import jax.numpy as jnp
from jax import lax
from jax.experimental import pallas as pl
from jax.experimental.pallas import tpu as pltpu
from jax.sharding import PartitionSpec as P

SOFT_CORE = 0.001
NEAR_RATE = 2.0
SCALE = 0.75 * math.log2(math.e)
SOFT = SCALE * SCALE * SOFT_CORE

LINE = 16
PLANE = 16
NEAR = 8
LANES = 128
GROUPS = 4
ROWS = 8 * GROUPS
STEPS = LANES // ROWS
PLAN = ((0,), (8,), (1,), (9,), (2,), (10, 3), (11,), (4,), (12, 5), (13,), (6,), (7,)) + ((),) * 4
ORDER = (0, 3, 1, 30, 10, 33, 31, 13, 11, 2, 20, 32, 12, 23, 21, 22)


def digits(unit):
    number = sum((step // unit % 10) << (2 * n) for n, step in enumerate(ORDER))
    return number - (1 << 32) if number >= 1 << 31 else number


ORDER_X, ORDER_Y = digits(10), digits(1)
MESH = pl.DeviceIdType.MESH
f32 = jnp.float32
bf16 = jnp.bfloat16


def split3(value):
    high = value.astype(bf16).astype(f32)
    rest = value - high
    mid = rest.astype(bf16).astype(f32)
    return high, mid, rest - mid


def kernel(
    tp_hbm,
    bnd_hbm,
    inv_hbm,
    ids_hbm,
    cnt_hbm,
    sp_hbm,
    area_hbm,
    hist_hbm,
    nt_hbm,
    out_ref,
    tp_ref,
    bnd_ref,
    inv_ref,
    ids_ref,
    cnt_ref,
    sp_ref,
    area_ref,
    hist_ref,
    nt_ref,
    in_sem,
    srcb,
    tgtb,
    nearb,
    part_send,
    part_recv,
    feat,
    lhs,
    rhs_s,
    rhs_p,
    xs,
    rows,
    soft_a,
    soft_b,
    proj_a,
    proj_b,
    wave_a,
    wave_b,
    acc_a,
    acc_b,
    res,
    nsel,
    xcol,
    nacc,
    line_send,
    line_recv,
    plane_send,
    plane_recv,
    near_send,
    near_recv,
    twin_send,
    twin_recv,
    back_send,
    back_recv,
):
    tgt, src = lax.axis_index("tgt"), lax.axis_index("src")
    z, x_hi, core = src >> 2, (src >> 1) & 1, src & 1
    me_line = z * 2 + core
    me_plane = tgt * 2 + x_hi

    def line_device(j):
        return (tgt, (j >> 1) * 4 + x_hi * 2 + (j & 1))

    def plane_device(i):
        return (i >> 1, z * 4 + (i & 1) * 2 + core)

    def line_peer(k):
        k2 = k >> 1
        off = ((k2 + 1) >> 1) * (2 * (k2 & 1) - 1)
        return ((z + off) & 7) * 2 + ((core + k) & 1)

    def plane_peer(k):
        x = (x_hi * 2 + (tgt >> 2) + ((ORDER_X >> (2 * k)) & 3)) & 3
        y = (tgt + ((ORDER_Y >> (2 * k)) & 3)) & 3
        return ((x & 1) * 4 + y) * 2 + (x >> 1)

    barrier = pltpu.get_barrier_semaphore()

    def greet(k, carry):
        pl.semaphore_signal(
            barrier, inc=1, device_id=line_device(line_peer(LINE - k)), device_id_type=MESH
        )
        pl.semaphore_signal(
            barrier, inc=1, device_id=plane_device(plane_peer(PLANE - k)), device_id_type=MESH
        )
        return carry

    lax.fori_loop(1, LINE, greet, 0)

    early = [(tp_hbm, tp_ref), (sp_hbm, sp_ref), (area_hbm, area_ref)]
    early += [(hist_hbm, hist_ref), (nt_hbm, nt_ref)]
    late = [(bnd_hbm, bnd_ref), (inv_hbm, inv_ref), (ids_hbm, ids_ref), (cnt_hbm, cnt_ref)]
    loads = [
        pltpu.make_async_copy(a, b, in_sem.at[n]) for n, (a, b) in enumerate(early + late)
    ]
    for load in loads:
        load.start()
    for load in loads[: len(early)]:
        load.wait()

    area = area_ref[...]
    srcb[me_plane, 0, 0:3, :] = sp_ref[...]
    h0, h1 = hist_ref[:, 0, :], hist_ref[:, 1, :]
    for a in range(3):
        mixed = jnp.sum(nt_ref[3 * a : 3 * a + 3, :] * h0, axis=0, keepdims=True)
        srcb[me_plane, 0, 3 + a : 4 + a, :] = area * mixed
    srcb[me_plane, 1, 0:3, :] = (area * h0) * SCALE
    srcb[me_plane, 1, 3:6, :] = (area * h1) * SCALE
    tgtb[me_line, 0:3, :] = tp_ref[...]

    def line_copy(slot, peer):
        return pltpu.make_async_remote_copy(
            src_ref=tgtb.at[slot, 0:3, :],
            dst_ref=tgtb.at[slot, 0:3, :],
            send_sem=line_send.at[peer],
            recv_sem=line_recv.at[slot],
            device_id=line_device(peer),
            device_id_type=MESH,
        )

    def plane_copy(slot, peer):
        return pltpu.make_async_remote_copy(
            src_ref=srcb.at[slot, :, 0:6, :],
            dst_ref=srcb.at[slot, :, 0:6, :],
            send_sem=plane_send.at[peer],
            recv_sem=plane_recv.at[slot],
            device_id=plane_device(peer),
            device_id_type=MESH,
        )

    def near_copy(at_z, peer_z):
        return pltpu.make_async_remote_copy(
            src_ref=srcb.at[:, 0, 0:6, :],
            dst_ref=nearb.at[core, at_z, :, 0:6, :],
            send_sem=near_send.at[peer_z],
            recv_sem=near_recv.at[at_z],
            device_id=(tgt, peer_z * 4 + x_hi * 2 + core),
            device_id_type=MESH,
        )

    def twin_copy(which):
        part = nearb.at[which, :, :, 0:6, :]
        return pltpu.make_async_remote_copy(
            src_ref=part,
            dst_ref=part,
            send_sem=twin_send,
            recv_sem=twin_recv,
            device_id=(tgt, z * 4 + x_hi * 2 + 1 - core),
            device_id_type=MESH,
        )

    def back_copy(block, slot):
        return pltpu.make_async_remote_copy(
            src_ref=part_send.at[block, 0:3, :],
            dst_ref=part_recv.at[slot, 0:3, :],
            send_sem=back_send.at[block],
            recv_sem=back_recv.at[slot],
            device_id=line_device(block),
            device_id_type=MESH,
        )

    def prep_target(s, n):
        x = (tgtb[s, 0:3, :] - 0.5) * SCALE
        high, mid, low = split3(x)
        n_high, n_mid, n_low = split3(jnp.sum(x * x, axis=0, keepdims=True))
        feat[4, 0:3, :] = high
        feat[4, 3:6, :] = high
        feat[4, 6:9, :] = high
        feat[4, 9:12, :] = mid
        feat[4, 12:15, :] = mid
        feat[4, 15:18, :] = low
        feat[4, 18:19, :] = n_high
        feat[4, 19:20, :] = n_mid
        feat[4, 20:21, :] = n_low
        feat[4, 21:24, :] = jnp.ones((3, LANES), f32)
        lhs[n] = feat[4].T.astype(bf16)
        xs[n, 0:3, :] = x

    def prep_source(s):
        y = (srcb[s, 0, 0:3, :] - 0.5) * SCALE
        one, zero = jnp.ones((3, LANES), f32), jnp.zeros((3, LANES), f32)
        piece, place = s >> 2, s & 3

        def put(number, dst, base, value, middle, tail):
            high, mid, low = split3(value)
            t_high, t_mid, t_low = split3(tail)
            feat[number, 0:3, :] = high
            feat[number, 3:6, :] = mid
            feat[number, 6:9, :] = low
            feat[number, 9:12, :] = high
            feat[number, 12:15, :] = mid
            feat[number, 15:18, :] = high
            feat[number, 18:21, :] = middle
            feat[number, 21:22, :] = t_high
            feat[number, 22:23, :] = t_mid
            feat[number, 23:24, :] = t_low
            dst[piece, :, pl.ds(pl.multiple_of(base, LANES), LANES)] = feat[number].astype(bf16)

        square = jnp.sum(y * y, axis=0, keepdims=True) + SOFT
        put(0, rhs_s, place * LANES, -2.0 * y, one, square)
        rows[s, 0:3, :] = y
        first, second = srcb[s, 1, 0:3, :], srcb[s, 1, 3:6, :]
        for n, dens in enumerate((0.5 * first, 0.5 * second - first, second)):
            tail = -jnp.sum(y * dens, axis=0, keepdims=True)
            put(n + 1, rhs_p, place * (3 * LANES) + n * LANES, dens, zero, tail)
        rows[s, 3:6, :] = first
        rows[s, 6:9, :] = second

    for n in range(5):
        feat[n, 24:32, :] = jnp.zeros((8, LANES), f32)
    prep_target(me_line, LINE - 1)
    prep_source(me_plane)
    for c in range(3):
        xcol[c] = jnp.broadcast_to(tp_ref[c : c + 1, :], (LANES, LANES)).T

    pl.semaphore_wait(barrier, LINE - 1 + PLANE - 1)

    def send(k, carry):
        plane_copy(me_plane, plane_peer(PLANE - k)).start()
        line_copy(me_line, line_peer(LINE - k)).start()
        return carry

    lax.fori_loop(1, LINE, send, 0)

    def prep(k, carry):
        i, j = plane_peer(k), line_peer(k)
        line_copy(j, j).wait_recv()
        prep_target(j, LINE - 1 - k)
        plane_copy(i, i).wait_recv()
        prep_source(i)
        return carry

    lax.fori_loop(1, LINE, prep, 0)

    def send_near(k, carry):
        near_copy(z, (z + k) & 7).start()
        return carry

    lax.fori_loop(1, 8, send_near, 0)

    def keep_near(i, carry):
        nearb[core, z, i, 0:6, :] = srcb[i, 0, 0:6, :]
        return carry

    lax.fori_loop(0, PLANE, keep_near, 0)

    def distances(dst, block, it, q):
        left = lhs[block, pl.ds(pl.multiple_of(it * ROWS, ROWS), ROWS), :]
        right = rhs_s[q // 2, :, 256 * (q % 2) : 256 * (q % 2) + 256]
        dst[q] = jnp.dot(left, right, preferred_element_type=f32)

    def projections(dst, block, piece, q):
        right = rhs_p[piece, :, 256 * q : 256 * q + 256]
        dst[piece, :, 256 * q : 256 * q + 256] = jnp.dot(
            lhs[block], right, preferred_element_type=f32
        )

    def waves(soft, dst, s):
        lo = LANES * (s % 2)
        for g in range(GROUPS):
            value = soft[s // 2, 8 * g : 8 * g + 8, lo : lo + LANES]
            inv = lax.rsqrt(value)
            dst[0, s, 8 * g : 8 * g + 8, :] = inv
            dst[1, s, 8 * g : 8 * g + 8, :] = jnp.exp2(-(value * inv))

    def add_source(wave_ref, proj, s, r0, total):
        row = [rows[s, pl.ds(r, 8, stride=0), :] for r in range(9)]
        for g in range(GROUPS):
            inv, wave = (wave_ref[n, s, 8 * g : 8 * g + 8, :] for n in range(2))
            lo = 3 * LANES * (s % 4)
            half, cross, second = (
                proj[s // 4, pl.ds(r0 + 8 * g, 8), lo + LANES * n : lo + LANES * (n + 1)]
                for n in range(3)
            )
            wave2 = wave * wave
            ratio = wave * inv
            amp = ratio * wave
            radial = (ratio * (inv * inv)) * (half + wave * (cross - wave2 * second))
            terms = [
                amp * (row[3 + c] + wave2 * row[6 + c]) - radial * row[c] for c in range(3)
            ]
            terms.append(radial)
            for c in range(4):
                old = total[g][c]
                total[g][c] = terms[c] if old is None else old + terms[c]

    def reduce_lanes(acc, c):
        res[c] = jnp.sum(acc[c].T, axis=0, keepdims=True)

    def block_of(n):
        return line_peer(LINE - 1 - n)

    def finish(n):
        block = block_of(n)
        for c in range(3):
            part_send[block, c : c + 1, :] = res[c] + xs[n, c : c + 1, :] * res[3]

    def unit(n, it, wave_now, wave_next, soft_now, soft_next, proj, following, acc, before):
        r0 = pl.multiple_of(it * ROWS, ROWS)
        ahead = jnp.minimum(n * STEPS + it + 2, LINE * STEPS - 1)
        block_2, it_2 = ahead >> 2, ahead & (STEPS - 1)
        block_1 = jnp.minimum(n + 1, LINE - 1)
        total = [[None] * 4 for _ in range(GROUPS)]
        pad = 4 + (n & 1)
        for s in range(PLANE):
            waves(soft_now, wave_next, s)
            if s > 0:
                rhs_s[pad, 0:16, 0:LANES] = jnp.concatenate(
                    [total[0][0], total[1][1]], axis=0
                ).astype(bf16)
                rhs_p[pad, 0:16, 0:LANES] = jnp.concatenate(
                    [total[2][2], total[3][0]], axis=0
                ).astype(bf16)
            for tile in PLAN[s]:
                if tile < 8:
                    distances(soft_next, block_2, it_2, tile)
                else:
                    projections(following, block_1, it, tile - 8)
            if s == 4:
                reduce_lanes(before, it)
            add_source(wave_now, proj, s, r0, total)
        for g in range(GROUPS):
            for c in range(4):
                acc[c, pl.ds(r0 + 8 * g, 8), :] = total[g][c]

    def block_step(n, proj, following, acc, before):
        def two_units(j, carry):
            unit(n, 2 * j, wave_a, wave_b, soft_b, soft_a, proj, following, acc, before)
            unit(n, 2 * j + 1, wave_b, wave_a, soft_a, soft_b, proj, following, acc, before)
            return carry

        lax.fori_loop(0, STEPS // 2, two_units, 0)

    def send_back(n):
        finish(n)
        back_copy(block_of(n), me_line).start()

    for q in range(8):
        distances(soft_a, 0, 0, q)
        distances(soft_b, 0, 1, q)
    for piece in range(4):
        for q in range(6):
            projections(proj_a, 0, piece, q)
    for s in range(PLANE):
        waves(soft_a, wave_a, s)

    def two(i, carry):
        block_step(2 * i, proj_a, proj_b, acc_a, acc_b)

        @pl.when(i > 0)
        def _():
            send_back(2 * i - 1)

        @pl.when(i == PLANE // 2 - 1)
        def _():
            for c in range(4):
                reduce_lanes(acc_a, c)
            send_back(2 * i)

        block_step(2 * i + 1, proj_b, proj_a, acc_b, acc_a)

        @pl.when(i < PLANE // 2 - 1)
        def _():
            send_back(2 * i)

        @pl.when(i == 5)
        def _():
            def landed(k, c):
                peer = (z + k) & 7
                near_copy(peer, peer).wait_recv()
                near_copy(z, peer).wait_send()
                return c

            lax.fori_loop(1, 8, landed, 0)

            def sent(k, c):
                plane_copy(me_plane, (me_plane + k) & (PLANE - 1)).wait_send()
                line_copy(me_line, (me_line + k) & (LINE - 1)).wait_send()
                return c

            lax.fori_loop(1, LINE, sent, 0)
            twin_copy(core).start()

        return carry

    lax.fori_loop(0, PLANE // 2, two, 0)
    for c in range(4):
        reduce_lanes(acc_b, c)
    finish(PLANE - 1)

    for load in loads[len(early) :]:
        load.wait()
    twin_copy(1 - core).wait_recv()
    for k in range(NEAR):
        listed = ids_ref[0, k]
        of_tgt, of_src = listed // 32, lax.rem(listed, 32)
        i = of_tgt * 2 + lax.rem(of_src // 2, 2)
        live = jnp.where(k < cnt_ref[0], 1.0, 0.0)
        piece = nearb[lax.rem(of_src, 2), of_src // 4, i, 0:6, :]
        nsel[k, 0:3, :] = piece[0:3]
        nsel[k, 3:6, :] = piece[3:6] * live

    def near_group(g, carry):
        r0 = pl.multiple_of(g * 8, 8)
        x = [xcol[c, pl.ds(r0, 8), :] for c in range(3)]
        total = [jnp.zeros((8, LANES), f32)] * 3
        for k in range(NEAR):
            row = [nsel[k, pl.ds(r, 8, stride=0), :] for r in range(6)]
            apart = [x[c] - row[c] for c in range(3)]
            square = apart[0] * apart[0] + apart[1] * apart[1] + apart[2] * apart[2]
            close = jnp.exp2(square * (-NEAR_RATE * math.log2(math.e)))
            total = [total[c] + close * row[3 + c] for c in range(3)]
        for c in range(3):
            nacc[c, pl.ds(r0, 8), :] = total[c]
        return carry

    lax.fori_loop(0, 16, near_group, 0)

    field = part_send[me_line, 0:3, :]
    near = [jnp.sum(nacc[c].T, axis=0, keepdims=True) for c in range(3)]

    def gather_back(k, total):
        peer = line_peer(k)
        back_copy(peer, peer).wait_recv()
        back_copy(peer, me_line).wait_send()
        return total + part_recv[peer, 0:3, :]

    field = lax.fori_loop(1, PLANE, gather_back, field)
    left = [bnd_ref[c : c + 1, :] - (field[c : c + 1, :] + near[c]) for c in range(3)]
    for a in range(3):
        out_ref[a : a + 1, :] = (
            inv_ref[a, 0:1, :] * left[0] + inv_ref[a, 1:2, :] * left[1]
        ) + inv_ref[a, 2:3, :] * left[2]
    twin_copy(core).wait_send()


def per_device(tp, bnd, inv, ids, cnt, sp, area, hist, nt):
    vmem = pl.BlockSpec(memory_space=pltpu.VMEM)
    hbm = pl.BlockSpec(memory_space=pltpu.HBM)
    dma = pltpu.SemaphoreType.DMA
    return pl.pallas_call(
        kernel,
        out_shape=jax.ShapeDtypeStruct((3, LANES), f32),
        in_specs=[hbm] * 9,
        out_specs=vmem,
        scratch_shapes=[
            pltpu.VMEM((3, LANES), f32),
            pltpu.VMEM((3, LANES), f32),
            pltpu.VMEM((3, 3, LANES), f32),
            pltpu.SMEM((1, NEAR), jnp.int32),
            pltpu.SMEM((1,), jnp.int32),
            pltpu.VMEM((3, LANES), f32),
            pltpu.VMEM((1, LANES), f32),
            pltpu.VMEM((3, 2, LANES), f32),
            pltpu.VMEM((9, LANES), f32),
            dma((9,)),
            pltpu.VMEM((LINE, 2, 8, LANES), f32),
            pltpu.VMEM((PLANE, 8, LANES), f32),
            pltpu.VMEM((2, 8, PLANE, 8, LANES), f32),
            pltpu.VMEM((PLANE, 8, LANES), f32),
            pltpu.VMEM((PLANE, 8, LANES), f32),
            pltpu.VMEM((5, 32, LANES), f32),
            pltpu.VMEM((PLANE, LANES, 32), bf16),
            pltpu.VMEM((6, 32, 4 * LANES), bf16),
            pltpu.VMEM((6, 32, 12 * LANES), bf16),
            pltpu.VMEM((PLANE, 8, LANES), f32),
            pltpu.VMEM((LINE, 16, LANES), f32),
            pltpu.VMEM((8, ROWS, 256), f32),
            pltpu.VMEM((8, ROWS, 256), f32),
            pltpu.VMEM((4, LANES, 12 * LANES), f32),
            pltpu.VMEM((4, LANES, 12 * LANES), f32),
            pltpu.VMEM((2, PLANE, ROWS, LANES), f32),
            pltpu.VMEM((2, PLANE, ROWS, LANES), f32),
            pltpu.VMEM((4, LANES, LANES), f32),
            pltpu.VMEM((4, LANES, LANES), f32),
            pltpu.VMEM((4, 1, LANES), f32),
            pltpu.VMEM((NEAR, 8, LANES), f32),
            pltpu.VMEM((3, LANES, LANES), f32),
            pltpu.VMEM((3, LANES, LANES), f32),
            dma((LINE,)),
            dma((LINE,)),
            dma((PLANE,)),
            dma((PLANE,)),
            dma((8,)),
            dma((8,)),
            dma,
            dma,
            dma((LINE,)),
            dma((LINE,)),
        ],
        compiler_params=pltpu.CompilerParams(
            collective_id=0, has_side_effects=True, vmem_limit_bytes=67043328
        ),
    )(
        tp, bnd, inv, ids, cnt, sp, area.reshape(1, LANES), hist.transpose(1, 0, 2), nt
    )


def solution(mesh):
    placed = (
        P(None, ("tgt", "src")),
        P(None, ("tgt", "src")),
        P(None, None, ("tgt", "src")),
        P(("tgt", "src"), None),
        P(("tgt", "src")),
        P(None, ("tgt", "src")),
        P(("tgt", "src")),
        P(None, None, ("tgt", "src")),
        P(None, ("tgt", "src")),
    )
    return jax.shard_map(
        per_device, mesh=mesh, in_specs=placed, out_specs=P(None, ("tgt", "src")), check_vma=False
    )
```

```python
import math

import jax
import jax.numpy as jnp
from jax import lax
from jax.experimental import pallas as pl
from jax.experimental.pallas import tpu as pltpu
from jax.sharding import PartitionSpec as P

SOFT_CORE = 0.001
NEAR_RATE = 2.0
SCALE = 0.75 * math.log2(math.e)
SOFT = SCALE * SCALE * SOFT_CORE

LINE = 16
PLANE = 16
NEAR = 8
LANES = 128
GROUPS = 4
ROWS = 8 * GROUPS
STEPS = LANES // ROWS
PLAN = ((0,), (8,), (1,), (9,), (2,), (10, 3), (11,), (4,), (12, 5), (13,), (6,), (7,)) + ((),) * 4
ORDER = (0, 3, 1, 30, 10, 33, 31, 13, 11, 2, 20, 32, 12, 23, 21, 22)


def digits(unit):
    number = sum((step // unit % 10) << (2 * n) for n, step in enumerate(ORDER))
    return number - (1 << 32) if number >= 1 << 31 else number


ORDER_X, ORDER_Y = digits(10), digits(1)
MESH = pl.DeviceIdType.MESH
f32 = jnp.float32
bf16 = jnp.bfloat16


def split3(value):
    high = value.astype(bf16).astype(f32)
    rest = value - high
    mid = rest.astype(bf16).astype(f32)
    return high, mid, rest - mid


def kernel(
    tp_hbm,
    bnd_hbm,
    inv_hbm,
    ids_hbm,
    cnt_hbm,
    sp_hbm,
    area_hbm,
    hist_hbm,
    nt_hbm,
    out_ref,
    tp_ref,
    bnd_ref,
    inv_ref,
    ids_ref,
    cnt_ref,
    sp_ref,
    area_ref,
    hist_ref,
    nt_ref,
    in_sem,
    srcb,
    tgtb,
    nearb,
    part_send,
    part_recv,
    feat,
    lhs,
    rhs_s,
    rhs_p,
    xs,
    rows,
    soft_a,
    soft_b,
    proj_a,
    proj_b,
    wave_a,
    wave_b,
    acc_a,
    acc_b,
    res,
    nsel,
    xcol,
    nacc,
    line_send,
    line_recv,
    plane_send,
    plane_recv,
    near_send,
    near_recv,
    twin_send,
    twin_recv,
    back_send,
    back_recv,
):
    tgt, src = lax.axis_index("tgt"), lax.axis_index("src")
    z, x_hi, core = src >> 2, (src >> 1) & 1, src & 1
    me_line = z * 2 + core
    me_plane = tgt * 2 + x_hi

    def line_device(j):
        return (tgt, (j >> 1) * 4 + x_hi * 2 + (j & 1))

    def plane_device(i):
        return (i >> 1, z * 4 + (i & 1) * 2 + core)

    def line_peer(k):
        k2 = k >> 1
        off = ((k2 + 1) >> 1) * (2 * (k2 & 1) - 1)
        return ((z + off) & 7) * 2 + ((core + k) & 1)

    def plane_peer(k):
        x = (x_hi * 2 + (tgt >> 2) + ((ORDER_X >> (2 * k)) & 3)) & 3
        y = (tgt + ((ORDER_Y >> (2 * k)) & 3)) & 3
        return ((x & 1) * 4 + y) * 2 + (x >> 1)

    barrier = pltpu.get_barrier_semaphore()

    def greet(k, carry):
        pl.semaphore_signal(
            barrier, inc=1, device_id=line_device(line_peer(LINE - k)), device_id_type=MESH
        )
        pl.semaphore_signal(
            barrier, inc=1, device_id=plane_device(plane_peer(PLANE - k)), device_id_type=MESH
        )
        return carry

    lax.fori_loop(1, LINE, greet, 0, unroll=3)

    early = [(tp_hbm, tp_ref), (sp_hbm, sp_ref), (area_hbm, area_ref)]
    early += [(hist_hbm, hist_ref), (nt_hbm, nt_ref)]
    late = [(bnd_hbm, bnd_ref), (inv_hbm, inv_ref), (ids_hbm, ids_ref), (cnt_hbm, cnt_ref)]
    loads = [
        pltpu.make_async_copy(a, b, in_sem.at[n]) for n, (a, b) in enumerate(early + late)
    ]
    for load in loads:
        load.start()
    for load in loads[: len(early)]:
        load.wait()

    area = area_ref[...]
    srcb[me_plane, 0, 0:3, :] = sp_ref[...]
    h0, h1 = hist_ref[:, 0, :], hist_ref[:, 1, :]
    for a in range(3):
        mixed = jnp.sum(nt_ref[3 * a : 3 * a + 3, :] * h0, axis=0, keepdims=True)
        srcb[me_plane, 0, 3 + a : 4 + a, :] = area * mixed
    srcb[me_plane, 1, 0:3, :] = (area * h0) * SCALE
    srcb[me_plane, 1, 3:6, :] = (area * h1) * SCALE
    tgtb[me_line, 0:3, :] = tp_ref[...]

    def line_copy(slot, peer):
        return pltpu.make_async_remote_copy(
            src_ref=tgtb.at[slot, 0:3, :],
            dst_ref=tgtb.at[slot, 0:3, :],
            send_sem=line_send.at[peer],
            recv_sem=line_recv.at[slot],
            device_id=line_device(peer),
            device_id_type=MESH,
        )

    def plane_copy(slot, peer):
        return pltpu.make_async_remote_copy(
            src_ref=srcb.at[slot, :, 0:6, :],
            dst_ref=srcb.at[slot, :, 0:6, :],
            send_sem=plane_send.at[peer],
            recv_sem=plane_recv.at[slot],
            device_id=plane_device(peer),
            device_id_type=MESH,
        )

    def near_copy(at_z, peer_z):
        return pltpu.make_async_remote_copy(
            src_ref=srcb.at[:, 0, 0:6, :],
            dst_ref=nearb.at[core, at_z, :, 0:6, :],
            send_sem=near_send.at[peer_z],
            recv_sem=near_recv.at[at_z],
            device_id=(tgt, peer_z * 4 + x_hi * 2 + core),
            device_id_type=MESH,
        )

    def twin_copy(which):
        part = nearb.at[which, :, :, 0:6, :]
        return pltpu.make_async_remote_copy(
            src_ref=part,
            dst_ref=part,
            send_sem=twin_send,
            recv_sem=twin_recv,
            device_id=(tgt, z * 4 + x_hi * 2 + 1 - core),
            device_id_type=MESH,
        )

    def back_copy(block, slot):
        return pltpu.make_async_remote_copy(
            src_ref=part_send.at[block, 0:3, :],
            dst_ref=part_recv.at[slot, 0:3, :],
            send_sem=back_send.at[block],
            recv_sem=back_recv.at[slot],
            device_id=line_device(block),
            device_id_type=MESH,
        )

    def prep_target(s, n, base=0):
        x = (tgtb[s, 0:3, :] - 0.5) * SCALE
        high, mid, low = split3(x)
        n_high, n_mid, n_low = split3(jnp.sum(x * x, axis=0, keepdims=True))
        feat[base + 4, 0:3, :] = high
        feat[base + 4, 3:6, :] = high
        feat[base + 4, 6:9, :] = high
        feat[base + 4, 9:12, :] = mid
        feat[base + 4, 12:15, :] = mid
        feat[base + 4, 15:18, :] = low
        feat[base + 4, 18:19, :] = n_high
        feat[base + 4, 19:20, :] = n_mid
        feat[base + 4, 20:21, :] = n_low
        feat[base + 4, 21:24, :] = jnp.ones((3, LANES), f32)
        lhs[n] = feat[base + 4].T.astype(bf16)
        xs[n, 0:3, :] = x

    def prep_source(s, first_feat=0):
        y = (srcb[s, 0, 0:3, :] - 0.5) * SCALE
        one, zero = jnp.ones((3, LANES), f32), jnp.zeros((3, LANES), f32)
        piece, place = s >> 2, s & 3

        def put(number, dst, base, value, middle, tail):
            number = first_feat + number
            high, mid, low = split3(value)
            t_high, t_mid, t_low = split3(tail)
            feat[number, 0:3, :] = high
            feat[number, 3:6, :] = mid
            feat[number, 6:9, :] = low
            feat[number, 9:12, :] = high
            feat[number, 12:15, :] = mid
            feat[number, 15:18, :] = high
            feat[number, 18:21, :] = middle
            feat[number, 21:22, :] = t_high
            feat[number, 22:23, :] = t_mid
            feat[number, 23:24, :] = t_low
            dst[piece, :, pl.ds(pl.multiple_of(base, LANES), LANES)] = feat[number].astype(bf16)

        square = jnp.sum(y * y, axis=0, keepdims=True) + SOFT
        put(0, rhs_s, place * LANES, -2.0 * y, one, square)
        rows[s, 0:3, :] = y
        first, second = srcb[s, 1, 0:3, :], srcb[s, 1, 3:6, :]
        for n, dens in enumerate((0.5 * first, 0.5 * second - first, second)):
            tail = -jnp.sum(y * dens, axis=0, keepdims=True)
            put(n + 1, rhs_p, place * (3 * LANES) + n * LANES, dens, zero, tail)
        rows[s, 3:6, :] = first
        rows[s, 6:9, :] = second

    for n in range(10):
        feat[n, 24:32, :] = jnp.zeros((8, LANES), f32)
    prep_target(me_line, LINE - 1)
    prep_source(me_plane)
    for c in range(3):
        xcol[c] = jnp.broadcast_to(tp_ref[c : c + 1, :], (LANES, LANES)).T

    pl.semaphore_wait(barrier, LINE - 1 + PLANE - 1)

    def send(k, carry):
        plane_copy(me_plane, plane_peer(PLANE - k)).start()
        line_copy(me_line, line_peer(LINE - k)).start()
        return carry

    lax.fori_loop(1, LINE, send, 0, unroll=3)

    def arrived(k):
        i, j = plane_peer(k), line_peer(k)
        line_copy(j, j).wait_recv()
        plane_copy(i, i).wait_recv()
        return i, j

    def prep_two(n, carry):
        k = 2 * n + 1
        (i_a, j_a), (i_b, j_b) = arrived(k), arrived(k + 1)
        prep_target(j_a, LINE - 1 - k)
        prep_target(j_b, LINE - 2 - k, 5)
        prep_source(i_a)
        prep_source(i_b, 5)
        return carry

    lax.fori_loop(0, (LINE - 1) // 2, prep_two, 0)
    i_last, j_last = arrived(LINE - 1)
    prep_target(j_last, 0)
    prep_source(i_last, 5)

    def send_near(k, carry):
        near_copy(z, (z + k) & 7).start()
        return carry

    lax.fori_loop(1, 8, send_near, 0)

    def keep_near(i, carry):
        nearb[core, z, i, 0:6, :] = srcb[i, 0, 0:6, :]
        return carry

    lax.fori_loop(0, PLANE, keep_near, 0)

    def distances(dst, block, it, q):
        left = lhs[block, pl.ds(pl.multiple_of(it * ROWS, ROWS), ROWS), :]
        right = rhs_s[q // 2, :, 256 * (q % 2) : 256 * (q % 2) + 256]
        dst[q] = jnp.dot(left, right, preferred_element_type=f32)

    def projections(dst, block, piece, q):
        right = rhs_p[piece, :, 256 * q : 256 * q + 256]
        dst[piece, :, 256 * q : 256 * q + 256] = jnp.dot(
            lhs[block], right, preferred_element_type=f32
        )

    def waves(soft, dst, s):
        lo = LANES * (s % 2)
        for g in range(GROUPS):
            value = soft[s // 2, 8 * g : 8 * g + 8, lo : lo + LANES]
            inv = lax.rsqrt(value)
            dst[0, s, 8 * g : 8 * g + 8, :] = inv
            dst[1, s, 8 * g : 8 * g + 8, :] = jnp.exp2(-(value * inv))

    def add_source(wave_ref, proj, s, r0, total):
        row = [rows[s, pl.ds(r, 8, stride=0), :] for r in range(9)]
        for g in range(GROUPS):
            inv, wave = (wave_ref[n, s, 8 * g : 8 * g + 8, :] for n in range(2))
            lo = 3 * LANES * (s % 4)
            half, cross, second = (
                proj[s // 4, pl.ds(r0 + 8 * g, 8), lo + LANES * n : lo + LANES * (n + 1)]
                for n in range(3)
            )
            wave2 = wave * wave
            ratio = wave * inv
            amp = ratio * wave
            radial = (ratio * (inv * inv)) * (half + wave * (cross - wave2 * second))
            terms = [
                amp * (row[3 + c] + wave2 * row[6 + c]) - radial * row[c] for c in range(3)
            ]
            terms.append(radial)
            for c in range(4):
                old = total[g][c]
                total[g][c] = terms[c] if old is None else old + terms[c]

    def reduce_lanes(acc, c):
        res[c] = jnp.sum(acc[c].T, axis=0, keepdims=True)

    def block_of(n):
        return line_peer(LINE - 1 - n)

    def finish(n):
        block = block_of(n)
        for c in range(3):
            part_send[block, c : c + 1, :] = res[c] + xs[n, c : c + 1, :] * res[3]

    def unit(n, it, wave_now, wave_next, soft_now, soft_next, proj, following, acc, before):
        r0 = pl.multiple_of(it * ROWS, ROWS)
        ahead = jnp.minimum(n * STEPS + it + 2, LINE * STEPS - 1)
        block_2, it_2 = ahead >> 2, ahead & (STEPS - 1)
        block_1 = jnp.minimum(n + 1, LINE - 1)
        total = [[None] * 4 for _ in range(GROUPS)]
        pad = 4 + (n & 1)
        for s in range(PLANE):
            waves(soft_now, wave_next, s)
            if s > 0:
                rhs_s[pad, 0:16, 0:LANES] = jnp.concatenate(
                    [total[0][0], total[1][1]], axis=0
                ).astype(bf16)
                rhs_p[pad, 0:16, 0:LANES] = jnp.concatenate(
                    [total[2][2], total[3][0]], axis=0
                ).astype(bf16)
            for tile in PLAN[s]:
                if tile < 8:
                    distances(soft_next, block_2, it_2, tile)
                else:
                    projections(following, block_1, it, tile - 8)
            if s == 4:
                reduce_lanes(before, it)
            add_source(wave_now, proj, s, r0, total)
        for g in range(GROUPS):
            for c in range(4):
                acc[c, pl.ds(r0 + 8 * g, 8), :] = total[g][c]

    def block_step(n, proj, following, acc, before):
        def two_units(j, carry):
            unit(n, 2 * j, wave_a, wave_b, soft_b, soft_a, proj, following, acc, before)
            unit(n, 2 * j + 1, wave_b, wave_a, soft_a, soft_b, proj, following, acc, before)
            return carry

        lax.fori_loop(0, STEPS // 2, two_units, 0)

    def send_back(n):
        finish(n)
        back_copy(block_of(n), me_line).start()

    for q in range(8):
        distances(soft_a, 0, 0, q)
        distances(soft_b, 0, 1, q)
    for piece in range(4):
        for q in range(6):
            projections(proj_a, 0, piece, q)
    for s in range(PLANE):
        waves(soft_a, wave_a, s)

    def two(i, carry):
        block_step(2 * i, proj_a, proj_b, acc_a, acc_b)

        @pl.when(i > 0)
        def _():
            send_back(2 * i - 1)

        @pl.when(i == PLANE // 2 - 1)
        def _():
            for c in range(4):
                reduce_lanes(acc_a, c)
            send_back(2 * i)

        block_step(2 * i + 1, proj_b, proj_a, acc_b, acc_a)

        @pl.when(i < PLANE // 2 - 1)
        def _():
            send_back(2 * i)

        @pl.when(i == 5)
        def _():
            def landed(k, c):
                peer = (z + k) & 7
                near_copy(peer, peer).wait_recv()
                near_copy(z, peer).wait_send()
                return c

            lax.fori_loop(1, 8, landed, 0)

            def sent(k, c):
                plane_copy(me_plane, (me_plane + k) & (PLANE - 1)).wait_send()
                line_copy(me_line, (me_line + k) & (LINE - 1)).wait_send()
                return c

            lax.fori_loop(1, LINE, sent, 0)
            twin_copy(core).start()

        return carry

    lax.fori_loop(0, PLANE // 2, two, 0)
    for c in range(4):
        reduce_lanes(acc_b, c)
    finish(PLANE - 1)

    for load in loads[len(early) :]:
        load.wait()
    twin_copy(1 - core).wait_recv()
    for k in range(NEAR):
        listed = ids_ref[0, k]
        of_tgt, of_src = listed // 32, lax.rem(listed, 32)
        i = of_tgt * 2 + lax.rem(of_src // 2, 2)
        live = jnp.where(k < cnt_ref[0], 1.0, 0.0)
        piece = nearb[lax.rem(of_src, 2), of_src // 4, i, 0:6, :]
        nsel[k, 0:3, :] = piece[0:3]
        nsel[k, 3:6, :] = piece[3:6] * live

    def near_group(g, carry):
        r0 = pl.multiple_of(g * 8, 8)
        x = [xcol[c, pl.ds(r0, 8), :] for c in range(3)]
        total = [jnp.zeros((8, LANES), f32)] * 3
        for k in range(NEAR):
            row = [nsel[k, pl.ds(r, 8, stride=0), :] for r in range(6)]
            apart = [x[c] - row[c] for c in range(3)]
            square = apart[0] * apart[0] + apart[1] * apart[1] + apart[2] * apart[2]
            close = jnp.exp2(square * (-NEAR_RATE * math.log2(math.e)))
            total = [total[c] + close * row[3 + c] for c in range(3)]
        for c in range(3):
            nacc[c, pl.ds(r0, 8), :] = total[c]
        return carry

    lax.fori_loop(0, 16, near_group, 0, unroll=4)

    field = part_send[me_line, 0:3, :]
    near = [jnp.sum(nacc[c].T, axis=0, keepdims=True) for c in range(3)]

    def gather_back(k, total):
        peer = line_peer(k)
        back_copy(peer, peer).wait_recv()
        back_copy(peer, me_line).wait_send()
        return total + part_recv[peer, 0:3, :]

    field = lax.fori_loop(1, PLANE, gather_back, field, unroll=3)
    left = [bnd_ref[c : c + 1, :] - (field[c : c + 1, :] + near[c]) for c in range(3)]
    for a in range(3):
        out_ref[a : a + 1, :] = (
            inv_ref[a, 0:1, :] * left[0] + inv_ref[a, 1:2, :] * left[1]
        ) + inv_ref[a, 2:3, :] * left[2]
    twin_copy(core).wait_send()


def per_device(tp, bnd, inv, ids, cnt, sp, area, hist, nt):
    vmem = pl.BlockSpec(memory_space=pltpu.VMEM)
    hbm = pl.BlockSpec(memory_space=pltpu.HBM)
    dma = pltpu.SemaphoreType.DMA
    return pl.pallas_call(
        kernel,
        out_shape=jax.ShapeDtypeStruct((3, LANES), f32),
        in_specs=[hbm] * 9,
        out_specs=vmem,
        scratch_shapes=[
            pltpu.VMEM((3, LANES), f32),
            pltpu.VMEM((3, LANES), f32),
            pltpu.VMEM((3, 3, LANES), f32),
            pltpu.SMEM((1, NEAR), jnp.int32),
            pltpu.SMEM((1,), jnp.int32),
            pltpu.VMEM((3, LANES), f32),
            pltpu.VMEM((1, LANES), f32),
            pltpu.VMEM((3, 2, LANES), f32),
            pltpu.VMEM((9, LANES), f32),
            dma((9,)),
            pltpu.VMEM((LINE, 2, 8, LANES), f32),
            pltpu.VMEM((PLANE, 8, LANES), f32),
            pltpu.VMEM((2, 8, PLANE, 8, LANES), f32),
            pltpu.VMEM((PLANE, 8, LANES), f32),
            pltpu.VMEM((PLANE, 8, LANES), f32),
            pltpu.VMEM((10, 32, LANES), f32),
            pltpu.VMEM((PLANE, LANES, 32), bf16),
            pltpu.VMEM((6, 32, 4 * LANES), bf16),
            pltpu.VMEM((6, 32, 12 * LANES), bf16),
            pltpu.VMEM((PLANE, 8, LANES), f32),
            pltpu.VMEM((LINE, 16, LANES), f32),
            pltpu.VMEM((8, ROWS, 256), f32),
            pltpu.VMEM((8, ROWS, 256), f32),
            pltpu.VMEM((4, LANES, 12 * LANES), f32),
            pltpu.VMEM((4, LANES, 12 * LANES), f32),
            pltpu.VMEM((2, PLANE, ROWS, LANES), f32),
            pltpu.VMEM((2, PLANE, ROWS, LANES), f32),
            pltpu.VMEM((4, LANES, LANES), f32),
            pltpu.VMEM((4, LANES, LANES), f32),
            pltpu.VMEM((4, 1, LANES), f32),
            pltpu.VMEM((NEAR, 8, LANES), f32),
            pltpu.VMEM((3, LANES, LANES), f32),
            pltpu.VMEM((3, LANES, LANES), f32),
            dma((LINE,)),
            dma((LINE,)),
            dma((PLANE,)),
            dma((PLANE,)),
            dma((8,)),
            dma((8,)),
            dma,
            dma,
            dma((LINE,)),
            dma((LINE,)),
        ],
        compiler_params=pltpu.CompilerParams(
            collective_id=0, has_side_effects=True, vmem_limit_bytes=67043328
        ),
    )(
        tp, bnd, inv, ids, cnt, sp, area.reshape(1, LANES), hist.transpose(1, 0, 2), nt
    )


def solution(mesh):
    placed = (
        P(None, ("tgt", "src")),
        P(None, ("tgt", "src")),
        P(None, None, ("tgt", "src")),
        P(("tgt", "src"), None),
        P(("tgt", "src")),
        P(None, ("tgt", "src")),
        P(("tgt", "src")),
        P(None, None, ("tgt", "src")),
        P(None, ("tgt", "src")),
    )
    return jax.shard_map(
        per_device, mesh=mesh, in_specs=placed, out_specs=P(None, ("tgt", "src")), check_vma=False
    )
```

```python
import math

import jax
import jax.numpy as jnp
from jax import lax
from jax.experimental import pallas as pl
from jax.experimental.pallas import tpu as pltpu
from jax.sharding import PartitionSpec as P

SOFT_CORE = 0.001
NEAR_RATE = 2.0
SCALE = 0.75 * math.log2(math.e)
SOFT = SCALE * SCALE * SOFT_CORE

LINE = 16
PLANE = 16
NEAR = 8
LANES = 128
GROUPS = 4
ROWS = 8 * GROUPS
STEPS = LANES // ROWS
PLAN = ((0,), (8,), (1,), (9,), (2,), (10, 3), (11,), (4,), (12, 5), (13,), (6,), (7,)) + ((),) * 4
ORDER = (0, 3, 1, 30, 10, 33, 31, 13, 11, 2, 20, 32, 12, 23, 21, 22)


def digits(unit):
    number = sum((step // unit % 10) << (2 * n) for n, step in enumerate(ORDER))
    return number - (1 << 32) if number >= 1 << 31 else number


ORDER_X, ORDER_Y = digits(10), digits(1)
MESH = pl.DeviceIdType.MESH
f32 = jnp.float32
bf16 = jnp.bfloat16


def split3(value):
    high = value.astype(bf16).astype(f32)
    rest = value - high
    mid = rest.astype(bf16).astype(f32)
    return high, mid, rest - mid


def kernel(
    tp_hbm,
    bnd_hbm,
    inv_hbm,
    ids_hbm,
    cnt_hbm,
    sp_hbm,
    area_hbm,
    hist_hbm,
    nt_hbm,
    out_ref,
    tp_ref,
    bnd_ref,
    inv_ref,
    ids_ref,
    cnt_ref,
    sp_ref,
    area_ref,
    hist_ref,
    nt_ref,
    in_sem,
    srcb,
    tgtb,
    nearb,
    part_send,
    part_recv,
    feat,
    lhs,
    rhs_s,
    rhs_p,
    xs,
    rows,
    soft_a,
    soft_b,
    proj_a,
    proj_b,
    wave_a,
    wave_b,
    acc_a,
    acc_b,
    res,
    nsel,
    xcol,
    nacc,
    line_send,
    line_recv,
    plane_send,
    plane_recv,
    near_send,
    near_recv,
    twin_send,
    twin_recv,
    back_send,
    back_recv,
):
    tgt, src = lax.axis_index("tgt"), lax.axis_index("src")
    z, x_hi, core = src >> 2, (src >> 1) & 1, src & 1
    me_line = z * 2 + core
    me_plane = tgt * 2 + x_hi

    def line_device(j):
        return (tgt, (j >> 1) * 4 + x_hi * 2 + (j & 1))

    def plane_device(i):
        return (i >> 1, z * 4 + (i & 1) * 2 + core)

    def line_peer(k):
        k2 = k >> 1
        off = ((k2 + 1) >> 1) * (2 * (k2 & 1) - 1)
        return ((z + off) & 7) * 2 + ((core + k) & 1)

    def plane_peer(k):
        x = (x_hi * 2 + (tgt >> 2) + ((ORDER_X >> (2 * k)) & 3)) & 3
        y = (tgt + ((ORDER_Y >> (2 * k)) & 3)) & 3
        return ((x & 1) * 4 + y) * 2 + (x >> 1)

    barrier = pltpu.get_barrier_semaphore()

    def greet(k, carry):
        pl.semaphore_signal(
            barrier, inc=1, device_id=line_device(line_peer(LINE - k)), device_id_type=MESH
        )
        pl.semaphore_signal(
            barrier, inc=1, device_id=plane_device(plane_peer(PLANE - k)), device_id_type=MESH
        )
        return carry

    lax.fori_loop(1, LINE, greet, 0, unroll=3)

    early = [(tp_hbm, tp_ref), (sp_hbm, sp_ref), (area_hbm, area_ref)]
    early += [(hist_hbm, hist_ref), (nt_hbm, nt_ref)]
    late = [(bnd_hbm, bnd_ref), (inv_hbm, inv_ref), (ids_hbm, ids_ref), (cnt_hbm, cnt_ref)]
    loads = [
        pltpu.make_async_copy(a, b, in_sem.at[n]) for n, (a, b) in enumerate(early + late)
    ]
    for load in loads:
        load.start()
    for load in loads[: len(early)]:
        load.wait()

    area = area_ref[...]
    srcb[me_plane, 0, 0:3, :] = sp_ref[...]
    h0, h1 = hist_ref[:, 0, :], hist_ref[:, 1, :]
    for a in range(3):
        mixed = jnp.sum(nt_ref[3 * a : 3 * a + 3, :] * h0, axis=0, keepdims=True)
        srcb[me_plane, 0, 3 + a : 4 + a, :] = area * mixed
    srcb[me_plane, 1, 0:3, :] = (area * h0) * SCALE
    srcb[me_plane, 1, 3:6, :] = (area * h1) * SCALE
    tgtb[me_line, 0:3, :] = tp_ref[...]

    def line_copy(slot, peer):
        return pltpu.make_async_remote_copy(
            src_ref=tgtb.at[slot, 0:3, :],
            dst_ref=tgtb.at[slot, 0:3, :],
            send_sem=line_send.at[peer],
            recv_sem=line_recv.at[slot],
            device_id=line_device(peer),
            device_id_type=MESH,
        )

    def plane_copy(slot, peer):
        return pltpu.make_async_remote_copy(
            src_ref=srcb.at[slot, :, 0:6, :],
            dst_ref=srcb.at[slot, :, 0:6, :],
            send_sem=plane_send.at[peer],
            recv_sem=plane_recv.at[slot],
            device_id=plane_device(peer),
            device_id_type=MESH,
        )

    def near_copy(at_z, peer_z):
        return pltpu.make_async_remote_copy(
            src_ref=srcb.at[:, 0, 0:6, :],
            dst_ref=nearb.at[core, at_z, :, 0:6, :],
            send_sem=near_send.at[peer_z],
            recv_sem=near_recv.at[at_z],
            device_id=(tgt, peer_z * 4 + x_hi * 2 + core),
            device_id_type=MESH,
        )

    def twin_copy(which):
        part = nearb.at[which, :, :, 0:6, :]
        return pltpu.make_async_remote_copy(
            src_ref=part,
            dst_ref=part,
            send_sem=twin_send,
            recv_sem=twin_recv,
            device_id=(tgt, z * 4 + x_hi * 2 + 1 - core),
            device_id_type=MESH,
        )

    def back_copy(block, slot):
        return pltpu.make_async_remote_copy(
            src_ref=part_send.at[block, 0:3, :],
            dst_ref=part_recv.at[slot, 0:3, :],
            send_sem=back_send.at[block],
            recv_sem=back_recv.at[slot],
            device_id=line_device(block),
            device_id_type=MESH,
        )

    def prep_target(s, n, base=0):
        x = (tgtb[s, 0:3, :] - 0.5) * SCALE
        high, mid, low = split3(x)
        n_high, n_mid, n_low = split3(jnp.sum(x * x, axis=0, keepdims=True))
        feat[base + 4, 0:3, :] = high
        feat[base + 4, 3:6, :] = high
        feat[base + 4, 6:9, :] = high
        feat[base + 4, 9:12, :] = mid
        feat[base + 4, 12:15, :] = mid
        feat[base + 4, 15:18, :] = low
        feat[base + 4, 18:19, :] = n_high
        feat[base + 4, 19:20, :] = n_mid
        feat[base + 4, 20:21, :] = n_low
        feat[base + 4, 21:24, :] = jnp.ones((3, LANES), f32)
        lhs[n] = feat[base + 4].T.astype(bf16)
        xs[n, 0:3, :] = x

    def prep_source(s, first_feat=0):
        y = (srcb[s, 0, 0:3, :] - 0.5) * SCALE
        one, zero = jnp.ones((3, LANES), f32), jnp.zeros((3, LANES), f32)
        piece, place = s >> 2, s & 3

        def put(number, dst, base, value, middle, tail):
            number = first_feat + number
            high, mid, low = split3(value)
            t_high, t_mid, t_low = split3(tail)
            feat[number, 0:3, :] = high
            feat[number, 3:6, :] = mid
            feat[number, 6:9, :] = low
            feat[number, 9:12, :] = high
            feat[number, 12:15, :] = mid
            feat[number, 15:18, :] = high
            feat[number, 18:21, :] = middle
            feat[number, 21:22, :] = t_high
            feat[number, 22:23, :] = t_mid
            feat[number, 23:24, :] = t_low
            dst[piece, :, pl.ds(pl.multiple_of(base, LANES), LANES)] = feat[number].astype(bf16)

        square = jnp.sum(y * y, axis=0, keepdims=True) + SOFT
        put(0, rhs_s, place * LANES, -2.0 * y, one, square)
        rows[s, 0:3, :] = y
        first, second = srcb[s, 1, 0:3, :], srcb[s, 1, 3:6, :]
        for n, dens in enumerate((0.5 * first, 0.5 * second - first, second)):
            tail = -jnp.sum(y * dens, axis=0, keepdims=True)
            put(n + 1, rhs_p, place * (3 * LANES) + n * LANES, dens, zero, tail)
        rows[s, 3:6, :] = first
        rows[s, 6:9, :] = second

    for n in range(10):
        feat[n, 24:32, :] = jnp.zeros((8, LANES), f32)
    prep_target(me_line, LINE - 1)
    prep_source(me_plane)
    for c in range(3):
        xcol[c] = jnp.broadcast_to(tp_ref[c : c + 1, :], (LANES, LANES)).T

    pl.semaphore_wait(barrier, LINE - 1 + PLANE - 1)

    def send(k, carry):
        plane_copy(me_plane, plane_peer(PLANE - k)).start()
        line_copy(me_line, line_peer(LINE - k)).start()
        return carry

    lax.fori_loop(1, LINE, send, 0, unroll=3)

    def arrived(k):
        i, j = plane_peer(k), line_peer(k)
        line_copy(j, j).wait_recv()
        plane_copy(i, i).wait_recv()
        return i, j

    def prep_two(n, carry):
        k = 2 * n + 1
        (i_a, j_a), (i_b, j_b) = arrived(k), arrived(k + 1)
        prep_target(j_a, LINE - 1 - k)
        prep_target(j_b, LINE - 2 - k, 5)
        prep_source(i_a)
        prep_source(i_b, 5)
        return carry

    lax.fori_loop(0, (LINE - 1) // 2, prep_two, 0)
    i_last, j_last = arrived(LINE - 1)
    prep_target(j_last, 0)
    prep_source(i_last, 5)

    def send_near(k, carry):
        near_copy(z, (z + k) & 7).start()
        return carry

    lax.fori_loop(1, 8, send_near, 0)

    def distances(dst, block, it, q):
        left = lhs[block, pl.ds(pl.multiple_of(it * ROWS, ROWS), ROWS), :]
        right = rhs_s[q // 2, :, 256 * (q % 2) : 256 * (q % 2) + 256]
        dst[q] = jnp.dot(left, right, preferred_element_type=f32)

    def projections(dst, block, piece, q):
        right = rhs_p[piece, :, 256 * q : 256 * q + 256]
        dst[piece, :, 256 * q : 256 * q + 256] = jnp.dot(
            lhs[block], right, preferred_element_type=f32
        )

    def waves(soft, dst, s):
        lo = LANES * (s % 2)
        for g in range(GROUPS):
            value = soft[s // 2, 8 * g : 8 * g + 8, lo : lo + LANES]
            inv = lax.rsqrt(value)
            dst[0, s, 8 * g : 8 * g + 8, :] = inv
            dst[1, s, 8 * g : 8 * g + 8, :] = jnp.exp2(-(value * inv))

    def add_source(wave_ref, proj, s, r0, total):
        row = [rows[s, pl.ds(r, 8, stride=0), :] for r in range(9)]
        for g in range(GROUPS):
            inv, wave = (wave_ref[n, s, 8 * g : 8 * g + 8, :] for n in range(2))
            lo = 3 * LANES * (s % 4)
            half, cross, second = (
                proj[s // 4, pl.ds(r0 + 8 * g, 8), lo + LANES * n : lo + LANES * (n + 1)]
                for n in range(3)
            )
            wave2 = wave * wave
            ratio = wave * inv
            amp = ratio * wave
            radial = (ratio * (inv * inv)) * (half + wave * (cross - wave2 * second))
            terms = [
                amp * (row[3 + c] + wave2 * row[6 + c]) - radial * row[c] for c in range(3)
            ]
            terms.append(radial)
            for c in range(4):
                old = total[g][c]
                total[g][c] = terms[c] if old is None else old + terms[c]

    def reduce_lanes(acc, c):
        res[c] = jnp.sum(acc[c].T, axis=0, keepdims=True)

    def block_of(n):
        return line_peer(LINE - 1 - n)

    def finish(n):
        block = block_of(n)
        for c in range(3):
            part_send[block, c : c + 1, :] = res[c] + xs[n, c : c + 1, :] * res[3]

    def unit(n, it, wave_now, wave_next, soft_now, soft_next, proj, following, acc, before):
        r0 = pl.multiple_of(it * ROWS, ROWS)
        ahead = jnp.minimum(n * STEPS + it + 2, LINE * STEPS - 1)
        block_2, it_2 = ahead >> 2, ahead & (STEPS - 1)
        block_1 = jnp.minimum(n + 1, LINE - 1)
        total = [[None] * 4 for _ in range(GROUPS)]
        pad = 4 + (n & 1)
        for s in range(PLANE):
            waves(soft_now, wave_next, s)
            if s > 0:
                rhs_s[pad, 0:16, 0:LANES] = jnp.concatenate(
                    [total[0][0], total[1][1]], axis=0
                ).astype(bf16)
                rhs_p[pad, 0:16, 0:LANES] = jnp.concatenate(
                    [total[2][2], total[3][0]], axis=0
                ).astype(bf16)
            for tile in PLAN[s]:
                if tile < 8:
                    distances(soft_next, block_2, it_2, tile)
                else:
                    projections(following, block_1, it, tile - 8)
            if s == 4:
                reduce_lanes(before, it)
            add_source(wave_now, proj, s, r0, total)
        for g in range(GROUPS):
            for c in range(4):
                acc[c, pl.ds(r0 + 8 * g, 8), :] = total[g][c]

    def block_step(n, proj, following, acc, before):
        def two_units(j, carry):
            unit(n, 2 * j, wave_a, wave_b, soft_b, soft_a, proj, following, acc, before)
            unit(n, 2 * j + 1, wave_b, wave_a, soft_a, soft_b, proj, following, acc, before)
            return carry

        lax.fori_loop(0, STEPS // 2, two_units, 0)

    def send_back(n):
        finish(n)
        back_copy(block_of(n), me_line).start()

    for q in range(8):
        distances(soft_a, 0, 0, q)
        distances(soft_b, 0, 1, q)
    for piece in range(4):
        for q in range(6):
            projections(proj_a, 0, piece, q)
    for s in range(PLANE):
        waves(soft_a, wave_a, s)

    def two(i, carry):
        block_step(2 * i, proj_a, proj_b, acc_a, acc_b)

        @pl.when(i > 0)
        def _():
            send_back(2 * i - 1)

        @pl.when(i == PLANE // 2 - 1)
        def _():
            for c in range(4):
                reduce_lanes(acc_a, c)
            send_back(2 * i)

        block_step(2 * i + 1, proj_b, proj_a, acc_b, acc_a)

        @pl.when(i < PLANE // 2 - 1)
        def _():
            send_back(2 * i)

        @pl.when(i == 5)
        def _():
            def landed(k, c):
                peer = (z + k) & 7
                near_copy(peer, peer).wait_recv()
                near_copy(z, peer).wait_send()
                return c

            lax.fori_loop(1, 8, landed, 0)

            def keep_near(slot, c):
                nearb[core, z, slot, 0:6, :] = srcb[slot, 0, 0:6, :]
                return c

            lax.fori_loop(0, PLANE, keep_near, 0, unroll=4)

            def sent(k, c):
                plane_copy(me_plane, (me_plane + k) & (PLANE - 1)).wait_send()
                line_copy(me_line, (me_line + k) & (LINE - 1)).wait_send()
                return c

            lax.fori_loop(1, LINE, sent, 0)
            twin_copy(core).start()

        return carry

    lax.fori_loop(0, PLANE // 2, two, 0)
    for c in range(4):
        reduce_lanes(acc_b, c)
    finish(PLANE - 1)

    for load in loads[len(early) :]:
        load.wait()
    twin_copy(1 - core).wait_recv()
    for k in range(NEAR):
        listed = ids_ref[0, k]
        of_tgt, of_src = listed // 32, lax.rem(listed, 32)
        i = of_tgt * 2 + lax.rem(of_src // 2, 2)
        live = jnp.where(k < cnt_ref[0], 1.0, 0.0)
        piece = nearb[lax.rem(of_src, 2), of_src // 4, i, 0:6, :]
        nsel[k, 0:3, :] = piece[0:3]
        nsel[k, 3:6, :] = piece[3:6] * live

    def near_group(g, carry):
        r0 = pl.multiple_of(g * 8, 8)
        x = [xcol[c, pl.ds(r0, 8), :] for c in range(3)]
        total = [jnp.zeros((8, LANES), f32)] * 3
        for k in range(NEAR):
            row = [nsel[k, pl.ds(r, 8, stride=0), :] for r in range(6)]
            apart = [x[c] - row[c] for c in range(3)]
            square = apart[0] * apart[0] + apart[1] * apart[1] + apart[2] * apart[2]
            close = jnp.exp2(square * (-NEAR_RATE * math.log2(math.e)))
            total = [total[c] + close * row[3 + c] for c in range(3)]
        for c in range(3):
            nacc[c, pl.ds(r0, 8), :] = total[c]
        return carry

    lax.fori_loop(0, 16, near_group, 0, unroll=4)

    field = part_send[me_line, 0:3, :]
    near = [jnp.sum(nacc[c].T, axis=0, keepdims=True) for c in range(3)]

    def gather_back(k, total):
        peer = line_peer(k)
        back_copy(peer, peer).wait_recv()
        back_copy(peer, me_line).wait_send()
        return total + part_recv[peer, 0:3, :]

    field = lax.fori_loop(1, PLANE, gather_back, field, unroll=3)
    left = [bnd_ref[c : c + 1, :] - (field[c : c + 1, :] + near[c]) for c in range(3)]
    for a in range(3):
        out_ref[a : a + 1, :] = (
            inv_ref[a, 0:1, :] * left[0] + inv_ref[a, 1:2, :] * left[1]
        ) + inv_ref[a, 2:3, :] * left[2]
    twin_copy(core).wait_send()


def per_device(tp, bnd, inv, ids, cnt, sp, area, hist, nt):
    vmem = pl.BlockSpec(memory_space=pltpu.VMEM)
    hbm = pl.BlockSpec(memory_space=pltpu.HBM)
    dma = pltpu.SemaphoreType.DMA
    return pl.pallas_call(
        kernel,
        out_shape=jax.ShapeDtypeStruct((3, LANES), f32),
        in_specs=[hbm] * 9,
        out_specs=vmem,
        scratch_shapes=[
            pltpu.VMEM((3, LANES), f32),
            pltpu.VMEM((3, LANES), f32),
            pltpu.VMEM((3, 3, LANES), f32),
            pltpu.SMEM((1, NEAR), jnp.int32),
            pltpu.SMEM((1,), jnp.int32),
            pltpu.VMEM((3, LANES), f32),
            pltpu.VMEM((1, LANES), f32),
            pltpu.VMEM((3, 2, LANES), f32),
            pltpu.VMEM((9, LANES), f32),
            dma((9,)),
            pltpu.VMEM((LINE, 2, 8, LANES), f32),
            pltpu.VMEM((PLANE, 8, LANES), f32),
            pltpu.VMEM((2, 8, PLANE, 8, LANES), f32),
            pltpu.VMEM((PLANE, 8, LANES), f32),
            pltpu.VMEM((PLANE, 8, LANES), f32),
            pltpu.VMEM((10, 32, LANES), f32),
            pltpu.VMEM((PLANE, LANES, 32), bf16),
            pltpu.VMEM((6, 32, 4 * LANES), bf16),
            pltpu.VMEM((6, 32, 12 * LANES), bf16),
            pltpu.VMEM((PLANE, 8, LANES), f32),
            pltpu.VMEM((LINE, 16, LANES), f32),
            pltpu.VMEM((8, ROWS, 256), f32),
            pltpu.VMEM((8, ROWS, 256), f32),
            pltpu.VMEM((4, LANES, 12 * LANES), f32),
            pltpu.VMEM((4, LANES, 12 * LANES), f32),
            pltpu.VMEM((2, PLANE, ROWS, LANES), f32),
            pltpu.VMEM((2, PLANE, ROWS, LANES), f32),
            pltpu.VMEM((4, LANES, LANES), f32),
            pltpu.VMEM((4, LANES, LANES), f32),
            pltpu.VMEM((4, 1, LANES), f32),
            pltpu.VMEM((NEAR, 8, LANES), f32),
            pltpu.VMEM((3, LANES, LANES), f32),
            pltpu.VMEM((3, LANES, LANES), f32),
            dma((LINE,)),
            dma((LINE,)),
            dma((PLANE,)),
            dma((PLANE,)),
            dma((8,)),
            dma((8,)),
            dma,
            dma,
            dma((LINE,)),
            dma((LINE,)),
        ],
        compiler_params=pltpu.CompilerParams(
            collective_id=0, has_side_effects=True, vmem_limit_bytes=67043328
        ),
    )(
        tp, bnd, inv, ids, cnt, sp, area.reshape(1, LANES), hist.transpose(1, 0, 2), nt
    )


def solution(mesh):
    placed = (
        P(None, ("tgt", "src")),
        P(None, ("tgt", "src")),
        P(None, None, ("tgt", "src")),
        P(("tgt", "src"), None),
        P(("tgt", "src")),
        P(None, ("tgt", "src")),
        P(("tgt", "src")),
        P(None, None, ("tgt", "src")),
        P(None, ("tgt", "src")),
    )
    return jax.shard_map(
        per_device, mesh=mesh, in_specs=placed, out_specs=P(None, ("tgt", "src")), check_vma=False
    )
```
